256 devices in a mesh: roll: 32 (over z_lo, x, core), tp: 8 (over z_hi, y).
Axes of the slice: x: 4, y: 4, z: 8 (z_hi: 2, z_lo: 4; z = z_hi * 4 + z_lo), core: 2. Of those that a mesh axis runs over, the one named last changes fastest.
Arguments:
- prompt_states: bfloat16 [32, 1024, 2048], P('roll', 'tp'), may hold values from -6 to 6
- lengths: int32 [32], P('roll'), may hold values from 256 to 1024, as said below
- bucket_owner: int32 [32], replicated, may hold values from 0 to 31, each once
- w_in: bfloat16 [2048, 6, 2048], P('roll', None, 'tp'), may hold values from -0.125 to 0.125
- w_gates: bfloat16 [2048, 2, 2, 16], P('roll', None, None, 'tp'), may hold values from -0.125 to 0.125
- out_weight: bfloat16 [2048, 2, 2048], P('roll', None, 'tp'), may hold values from -0.09375 to 0.09375
- conv_weight: bfloat16 [4, 4, 2048], P(None, None, 'tp'), may hold values from -3 to 3
- decay_rate: float32 [2, 16], P(None, 'tp'), may hold values from 0.001 to 0.05
- dt_bias: float32 [2, 16], P(None, 'tp'), may hold values from -3 to 3
- in_gain: float32 [2048], replicated, may hold values from 0.5 to 1.5
- head_gain: float32 [128], replicated, may hold values from 0.5 to 1.5
Outputs:
- layer_out: bfloat16 [32, 1024, 2048], P('roll', 'tp')
The draws below stay inside these ranges and needn't reach their ends.
Inputs may be any that keep to these rules, and one draw needn't show every extreme that they name: `lengths`: every prompt has at least 256 live positions, and some prompt has all 1024. `bucket_owner`: A permutation of the 32 row blocks.
All inputs are finite; a program needn't handle non-finite values.
Results may differ from the reference program's by a relative error of at most 0.015.
Values may be sent and summed in bfloat16 or wider, within the bound.
A program may use at most 64 MiB of HBM per device.

```python
import math
import jax
import jax.numpy as jnp
from jax import lax

D = 2048
KH = 16
DH = 128
CONV = 4
BLOCK = 64
KD = 2048
SEQ = 1024
PROMPTS = 32
BUCKETS = 32
N_TP = 8


def draw_lengths(key, part):
    drawn = jax.random.randint(key, (PROMPTS,), SEQ // 4, SEQ + 1, dtype=jnp.int32)
    chosen = jax.random.randint(jax.random.fold_in(key, 7), (), 0, PROMPTS, dtype=jnp.int32)
    return drawn.at[chosen].set(SEQ)


def block_levels(own_key, dims, cuts, smallest, top_value):
    gain, own = 1.0, jax.random.fold_in(own_key, 6)
    for position, blocks in cuts:
        steps = jnp.exp(jax.random.uniform(jax.random.fold_in(own, position), (blocks,), jnp.float32, smallest / len(cuts), top_value / len(cuts)))
        gain = gain * jnp.repeat(steps, dims[position] // blocks).reshape([-1 if axis == position else 1 for axis in range(len(dims))])
    return gain


def scatter_about(key, extent, deviation, bound, cuts=(), kind=jnp.bfloat16):
    entries = jax.random.normal(key, extent, jnp.float32) * deviation
    if len(cuts) > 0:
        entries = block_levels(key, extent, cuts, -0.22, 0.18) * entries
    return jnp.clip(entries, min=-bound, max=bound).astype(kind)


def setup_inputs(seed: int = 0) -> dict:
    splits = jax.random.split(jax.random.key(seed), 12)
    prompt_states = scatter_about(splits[0], (PROMPTS, SEQ, D), 1.0, 6.0, ((0, 32), (1, 8)))
    lengths = draw_lengths(jax.random.fold_in(splits[11], 71), 0)
    bucket_owner = jax.random.permutation(splits[2], BUCKETS).astype(jnp.int32)
    w_in = scatter_about(splits[3], (D, 6, KD), D ** -0.5, 0.125, ((0, 32), (2, 8)))
    w_gates = scatter_about(splits[4], (D, 2, 2, KH), D ** -0.5, 0.125, ((0, 32), (3, 8)))
    out_weight = scatter_about(splits[5], (D, 2, KD), (2 * KD) ** -0.5, 0.09375, ((0, 32), (2, 8)))
    conv_weight = scatter_about(splits[6], (CONV, 4, KD), CONV ** -0.5, 3.0, ((2, 8),))
    decay_rate = jnp.clip(jnp.exp(math.log(0.05) - 3.912023 * jax.random.uniform(splits[7], (2, KH), jnp.float32) ** block_levels(splits[7], (2, KH), ((1, 8),), -0.2, 0.2)), 0.001, 0.05)
    dt_bias = scatter_about(splits[8], (2, KH), 1.0, 3.0, ((1, 8),), jnp.float32)
    in_gain = jnp.clip(1.0 + 0.1 * jax.random.normal(splits[9], (D,), jnp.float32), 0.5, 1.5)
    head_gain = jnp.clip(1.0 + 0.1 * jax.random.normal(splits[10], (DH,), jnp.float32), 0.5, 1.5)
    return {"prompt_states": prompt_states, "lengths": lengths, "bucket_owner": bucket_owner, "w_in": w_in, "w_gates": w_gates, "out_weight": out_weight, "conv_weight": conv_weight, "decay_rate": decay_rate, "dt_bias": dt_bias, "in_gain": in_gain, "head_gain": head_gain}


HIGH = lax.Precision.HIGHEST

def delta_blocks(query, keys, values, decay, beta):
    heads_n, seq_len, depth = query.shape
    count = seq_len // BLOCK

    def split(array):
        return array.reshape((heads_n, count, BLOCK) + array.shape[2:]).swapaxes(0, 1)
    offsets = jnp.arange(BLOCK, dtype=jnp.int32)
    strict = offsets[:, None] > offsets[None, :]
    within = offsets[:, None] >= offsets[None, :]
    identity = jnp.eye(BLOCK, dtype=jnp.float32)

    def advance(state, blocks):
        block_q, block_k, block_v, block_g, block_b = blocks
        totals = jnp.cumsum(block_g, axis=-1)
        spans = totals[:, :, None] - totals[:, None, :]
        inside = jnp.where(within, jnp.exp(jnp.where(within, spans, 0.0)), 0.0)
        below = jnp.where(strict, inside, 0.0)
        key_key = jnp.einsum('hid,hjd->hij', block_k, block_k, precision=HIGH)
        system = identity + block_b[:, :, None] * key_key * below
        growth = jnp.exp(totals)
        right_side = jnp.concatenate([block_b[..., None] * block_v, (block_b * growth)[..., None] * block_k], axis=-1)
        solved = lax.linalg.triangular_solve(system, right_side, left_side=True, lower=True, unit_diagonal=True)
        update = solved[..., :depth] - jnp.einsum('hid,hde->hie', solved[..., depth:], state, precision=HIGH)
        scores = jnp.einsum('hid,hjd->hij', block_q, block_k, precision=HIGH) * inside
        outputs = growth[..., None] * jnp.einsum('hid,hde->hie', block_q, state, precision=HIGH)
        outputs = outputs + jnp.einsum('hij,hje->hie', scores, update, precision=HIGH)
        final_sum = totals[:, -1:]
        carry_weight = jnp.exp(final_sum - totals)
        new_state = jnp.exp(final_sum)[:, :, None] * state
        new_state = new_state + jnp.einsum('hjd,hje->hde', block_k * carry_weight[..., None], update, precision=HIGH)
        return (new_state, outputs)
    start_state = jnp.zeros((heads_n, depth, depth), jnp.float32)
    _, outs = lax.scan(advance, start_state, (split(query), split(keys), split(values), split(decay), split(beta)))
    return outs.swapaxes(0, 1).reshape(heads_n, seq_len, depth)

def unit_rows(array):
    return array / jnp.sqrt(lax.optimization_barrier(jnp.sum(array * array, axis=-1, keepdims=True)) + 1e-06)

def causal_conv(parts, taps):
    seq_len = parts.shape[0]
    width = taps.shape[0]
    padded = jnp.pad(parts, ((width - 1, 0), (0, 0), (0, 0), (0, 0)))
    total = jnp.zeros(parts.shape, jnp.float32)
    for shift_by in range(width):
        begin = width - 1 - shift_by
        total = total + taps[shift_by] * padded[begin:begin + seq_len]
    return total

def mixer(projected, gate_logits, conv_weight, decay_rate, dt_bias, head_gain, heads, head_dim):
    seq_len = projected.shape[0]
    parts = projected.reshape(seq_len, 6, heads, head_dim)
    taps = conv_weight.astype(jnp.float32).reshape(conv_weight.shape[0], 4, heads, head_dim)
    mixed = jax.nn.silu(causal_conv(parts[:, :4], taps))
    query = unit_rows(mixed[:, 0]) * head_dim ** (-0.5)
    keys = unit_rows(mixed[:, 1])
    values = mixed[:, 2:4]
    gates = gate_logits.reshape(seq_len, 2, 2, heads)
    beta = jax.nn.sigmoid(gates[:, 1])
    decay = -decay_rate * jax.nn.softplus(gates[:, 0] + dt_bias)
    value_heads = 2 * heads
    values_h = values.transpose(1, 2, 0, 3).reshape(value_heads, seq_len, head_dim)
    query_h = jnp.broadcast_to(query.transpose(1, 0, 2)[None], (2, heads, seq_len, head_dim)).reshape(value_heads, seq_len, head_dim)
    keys_h = jnp.broadcast_to(keys.transpose(1, 0, 2)[None], (2, heads, seq_len, head_dim)).reshape(value_heads, seq_len, head_dim)
    decay_h = decay.transpose(1, 2, 0).reshape(value_heads, seq_len)
    beta_h = beta.transpose(1, 2, 0).reshape(value_heads, seq_len)
    recur = delta_blocks(query_h, keys_h, values_h, decay_h, beta_h)
    recur = recur.reshape(2, heads, seq_len, head_dim).transpose(2, 0, 1, 3)
    normed = recur / jnp.sqrt(lax.optimization_barrier(jnp.mean(recur * recur, axis=-1, keepdims=True)) + 1e-06) * head_gain
    return (normed * jax.nn.silu(parts[:, 4:6])).astype(jnp.bfloat16)

def reference(prompt_states, lengths, bucket_owner, w_in, w_gates, out_weight, conv_weight, decay_rate, dt_bias, in_gain, head_gain):
    block_rows = D // BUCKETS

    def order(weight):
        blocks = weight.reshape((BUCKETS, block_rows) + weight.shape[1:])
        return jnp.take(blocks, bucket_owner.astype(jnp.int32), axis=0).reshape(weight.shape)
    in_true = order(w_in).reshape(D, 6 * KD)
    gates_true = order(w_gates).reshape(D, 4 * KH)
    out_true = order(out_weight).astype(jnp.float32).reshape(D, 2, N_TP, KD // N_TP)
    group_heads = KH // N_TP

    def one_prompt(pair):
        states, length = pair
        rows = states.astype(jnp.float32)
        normed = (rows / jnp.sqrt(lax.optimization_barrier(jnp.mean(rows * rows, axis=-1, keepdims=True)) + 1e-06) * in_gain).astype(jnp.bfloat16)
        projected = jnp.dot(normed.astype(jnp.float32), in_true.astype(jnp.float32), preferred_element_type=jnp.float32)
        gate_logits = jnp.dot(normed.astype(jnp.float32), gates_true.astype(jnp.float32), preferred_element_type=jnp.float32)
        hidden = mixer(projected, gate_logits, conv_weight, decay_rate, dt_bias, head_gain, KH, DH)
        grouped = hidden.astype(jnp.float32).reshape(SEQ, 2, N_TP, group_heads * DH)
        partial_value = jnp.einsum('tsgc,dsgc->gtd', grouped, out_true, precision=HIGH).astype(jnp.bfloat16)
        partial_value = lax.optimization_barrier(partial_value)
        summed = lax.optimization_barrier(jnp.sum(partial_value.astype(jnp.float32), axis=0))
        live = jnp.arange(SEQ, dtype=jnp.int32) < length
        return jnp.where(live[:, None], summed, 0.0).astype(jnp.bfloat16)
    return lax.map(one_prompt, (prompt_states, lengths))
```

```python
import jax
import jax.numpy as jnp
from jax import lax
from jax.experimental import pallas as pl
from jax.experimental.pallas import tpu as pltpu
from jax.sharding import PartitionSpec as P

CH = 64
NG = 4
ROWS = CH * NG
F32 = jnp.float32
BF16 = jnp.bfloat16
HIGHEST = lax.Precision.HIGHEST


def mm(a, b):
    return jnp.dot(a, b, preferred_element_type=F32)


def mm_nt(a, b):
    return lax.dot_general(a, b, (((1,), (1,)), ((), ())), preferred_element_type=F32)


def mm_tn(a, b):
    return lax.dot_general(a, b, (((0,), (0,)), ((), ())), preferred_element_type=F32)


def mm_exact(a, b):
    return jnp.dot(a, b, preferred_element_type=F32, precision=HIGHEST)


def silu(v):
    return v / (1.0 + jnp.exp(-v))


def mixer_kernel(x_ref, w_ref, taps_ref, rate_ref, bias_ref, gain_ref, out_ref, pscr, oscr, state):
    step = pl.program_id(0)

    @pl.when(step == 0)
    def _():
        pscr[0:8, :] = jnp.zeros((8, 1024), F32)
        state[...] = jnp.zeros_like(state)

    @pl.when(step > 0)
    def _():
        pscr[0:8, :] = pscr[ROWS : ROWS + 8, :]

    x = x_ref[...]
    gates = mm(x, w_ref[:, 1536:1664])
    pscr[8 : 8 + ROWS, :] = mm(x, w_ref[:, 0:1024])

    biased = gates + bias_ref[...]
    soft = jnp.maximum(biased, 0.0) + jnp.log(1.0 + jnp.exp(-jnp.abs(biased)))
    decay = -rate_ref[...] * soft
    beta = 1.0 / (1.0 + jnp.exp(-gates))
    ri = lax.broadcasted_iota(jnp.int32, (ROWS, ROWS), 0)
    ci = lax.broadcasted_iota(jnp.int32, (ROWS, ROWS), 1)
    same = (ri // CH) == (ci // CH)
    tri = jnp.where(same & (ri >= ci), 1.0, 0.0)
    totals = mm_exact(tri, decay)
    lane_r = lax.broadcasted_iota(jnp.int32, (128, 256), 0)
    lane_c = lax.broadcasted_iota(jnp.int32, (128, 256), 1)
    spread = jnp.where(lane_r == lane_c // CH, 1.0, 0.0)
    spread_b = jnp.where(lane_r == lane_c // CH + 4, 1.0, 0.0)
    lane_r5 = lax.broadcasted_iota(jnp.int32, (128, 512), 0)
    lane_c5 = lax.broadcasted_iota(jnp.int32, (128, 512), 1)
    spread5 = jnp.where(lane_r5 == lane_c5 // 128, 1.0, 0.0)
    spread5_b = jnp.where(lane_r5 == lane_c5 // 128 + 4, 1.0, 0.0)
    tot_w = mm_exact(totals, spread)
    beta_w = mm_exact(beta, spread_b)
    tot_v = mm_exact(totals, spread5)
    beta_v = mm_exact(beta, spread5_b)
    grow_v = jnp.exp(tot_v)

    mixed = []
    for c in range(4):
        acc = None
        for i in range(4):
            term = taps_ref[i : i + 1, c * 256 : (c + 1) * 256] * pscr[8 - i : 8 - i + ROWS, c * 256 : (c + 1) * 256]
            acc = term if acc is None else acc + term
        mixed.append(silu(acc))

    def unit(v):
        parts = []
        for h in range(2):
            p = v[:, h * 128 : (h + 1) * 128]
            parts.append(p * lax.rsqrt(jnp.sum(p * p, axis=-1, keepdims=True) + 1e-6))
        return jnp.concatenate(parts, axis=1)

    query = (unit(mixed[0]) * (128.0 ** -0.5)).astype(BF16)
    keys_f = unit(mixed[1])
    keys = keys_f.astype(BF16)

    wi = lax.broadcasted_iota(jnp.int32, (CH, 256), 0)
    wj = lax.broadcasted_iota(jnp.int32, (CH, 256), 1) % CH
    eye = wi == wj
    lower = wi >= wj
    strict = wi > wj
    bd_mask = same
    kmask = (lax.broadcasted_iota(jnp.int32, (128, 256), 0) // CH) == (
        lax.broadcasted_iota(jnp.int32, (128, 256), 1) // 128
    )

    def bd(v):
        vb = v.astype(BF16)
        return jnp.where(bd_mask, jnp.concatenate([vb] * 4, axis=0), jnp.zeros((), BF16))

    chunks = range(NG)
    rows = [slice(c * CH, (c + 1) * CH) for c in chunks]
    sys_w, score_w = [], []
    for c in chunks:
        k_c, q_c = keys[rows[c]], query[rows[c]]
        k_bd = jnp.where(kmask, jnp.concatenate([k_c, k_c], axis=0), jnp.zeros((), BF16))
        both = mm_nt(jnp.concatenate([k_c, q_c], axis=0), k_bd)
        kk = jnp.concatenate([both[:CH], both[:CH]], axis=1)
        qk = jnp.concatenate([both[CH:], both[CH:]], axis=1)
        t_c = tot_w[rows[c]]
        t_row = jnp.sum(jnp.where(eye, t_c, 0.0), axis=0, keepdims=True)
        inside = jnp.where(lower, jnp.exp(jnp.where(lower, t_c - t_row, 0.0)), 0.0)
        sys_w.append(jnp.where(strict, beta_w[rows[c]] * kk * inside, 0.0))
        score_w.append(qk * inside)

    eye_f = jnp.where(eye, 1.0, 0.0)

    def block(n):
        return (wi // n) == (wj // n)

    base = [jnp.where(block(8), a, 0.0) for a in sys_w]
    base2 = [mm(d.astype(BF16), bd(d)) for d in base]
    base4 = [mm(d.astype(BF16), bd(d)) for d in base2]
    inv = [eye_f - d for d in base]
    inv = [t + mm(t.astype(BF16), bd(d)) for t, d in zip(inv, base2)]
    inv = [t + mm(t.astype(BF16), bd(d)) for t, d in zip(inv, base4)]
    for n in (16, 32, 64):
        pick = block(n) & jnp.logical_not(block(n // 2))
        low = [jnp.where(pick, a, 0.0).astype(BF16) for a in sys_w]
        mid = [mm(l, bd(t)) for l, t in zip(low, inv)]
        inv = [t - mm(t.astype(BF16), bd(m)) for t, m in zip(inv, mid)]
    fixed = []
    for c in chunks:
        a_hi = sys_w[c].astype(BF16)
        a_lo = (sys_w[c] - a_hi.astype(F32)).astype(BF16)
        t_hi = inv[c].astype(BF16)
        t_lo = (inv[c] - t_hi.astype(F32)).astype(BF16)
        both = mm(jnp.concatenate([a_hi, a_lo], axis=0), bd(t_hi))
        prod = both[:CH] + both[CH:] + mm(a_hi, bd(t_lo))
        resid = eye_f - inv[c] - prod
        fixed.append(inv[c] + mm(t_hi, bd(resid)))
    inv = fixed

    solved = []
    for c in chunks:
        parts = []
        for s in range(2):
            for h in range(2):
                n = s * 2 + h
                b = beta_v[rows[c], n * 128 : (n + 1) * 128]
                g = grow_v[rows[c], n * 128 : (n + 1) * 128]
                v = mixed[2 + s][rows[c], h * 128 : (h + 1) * 128]
                k = keys_f[rows[c], h * 128 : (h + 1) * 128]
                parts.append(jnp.concatenate([(b * v).astype(BF16), (b * g * k).astype(BF16)], axis=1))
        rhs = jnp.concatenate(parts, axis=0)
        solved.append(mm(bd(inv[c]), rhs))
    score_bd = [bd(s) for s in score_w]

    for c in chunks:
        reads = []
        for h in range(2):
            lhs = jnp.concatenate(
                [
                    solved[c][h * CH : (h + 1) * CH, 128:256].astype(BF16),
                    solved[c][(2 + h) * CH : (3 + h) * CH, 128:256].astype(BF16),
                    query[rows[c], h * 128 : (h + 1) * 128],
                ],
                axis=0,
            )
            reads.append(mm(lhs, state[h].astype(BF16)))
        updates, writes = [None] * 4, [None] * 4
        last = tot_v[(c + 1) * CH - 1 : (c + 1) * CH, :]
        for s in range(2):
            for h in range(2):
                n = s * 2 + h
                u = solved[c][n * CH : (n + 1) * CH, 0:128] - reads[h][s * CH : (s + 1) * CH, s * 128 : (s + 1) * 128]
                carry = jnp.exp(last[:, n * 128 : (n + 1) * 128] - tot_v[rows[c], n * 128 : (n + 1) * 128])
                updates[n] = u.astype(BF16)
                writes[n] = (carry * u).astype(BF16)
        for h in range(2):
            decay_all = jnp.concatenate(
                [jnp.exp(last[:, h * 128 : (h + 1) * 128]), jnp.exp(last[:, (2 + h) * 128 : (3 + h) * 128])], axis=1
            )
            write = jnp.concatenate([writes[h], writes[2 + h]], axis=1)
            state[h] = decay_all * state[h] + mm_tn(keys[rows[c], h * 128 : (h + 1) * 128], write)
        inner = mm(score_bd[c], jnp.concatenate(updates, axis=0))
        for s in range(2):
            for h in range(2):
                n = s * 2 + h
                oscr[rows[c], n * 128 : (n + 1) * 128] = (
                    grow_v[rows[c], n * 128 : (n + 1) * 128] * reads[h][2 * CH :, s * 128 : (s + 1) * 128]
                    + inner[n * CH : (n + 1) * CH]
                )

    og = mm(x, w_ref[:, 1024:1536])
    hidden = []
    for n in range(4):
        r = oscr[:, n * 128 : (n + 1) * 128]
        r = r * lax.rsqrt(jnp.mean(r * r, axis=-1, keepdims=True) + 1e-6) * gain_ref[...]
        hidden.append((r * silu(og[:, n * 128 : (n + 1) * 128])).astype(BF16))
    hidden = jnp.concatenate(hidden, axis=1)
    out_ref[...] = mm_nt(hidden, w_ref[:, 1664:2176]).astype(BF16)


def mixer(x, w, taps, rate, bias, gain):
    seq = x.shape[0]
    return pl.pallas_call(
        mixer_kernel,
        grid=(seq // ROWS,),
        out_shape=jax.ShapeDtypeStruct((seq, 2048), BF16),
        in_specs=[
            pl.BlockSpec((ROWS, 2048), lambda i: (i, 0)),
            pl.BlockSpec((2048, 2176), lambda i: (0, 0), pipeline_mode=pl.Buffered(1)),
            pl.BlockSpec((4, 1024), lambda i: (0, 0)),
            pl.BlockSpec((1, 128), lambda i: (0, 0)),
            pl.BlockSpec((1, 128), lambda i: (0, 0)),
            pl.BlockSpec((1, 128), lambda i: (0, 0)),
        ],
        out_specs=pl.BlockSpec((ROWS, 2048), lambda i: (i, 0)),
        scratch_shapes=[
            pltpu.VMEM((ROWS + 8, 1024), F32),
            pltpu.VMEM((ROWS, 512), F32),
            pltpu.VMEM((2, 128, 256), F32),
        ],
        compiler_params=pltpu.CompilerParams(vmem_limit_bytes=48 << 20),
        name="mixer",
    )(x, w, taps, rate, bias, gain)


def prep_kernel(owner_ref, x_ref, gain_ref, out_ref, scr, inverse):
    x = x_ref[...].astype(F32)
    scale = lax.rsqrt(jnp.mean(x * x, axis=-1, keepdims=True) + 1e-6)
    scr[...] = x * scale * gain_ref[...]
    for b in range(32):
        inverse[owner_ref[b]] = b
    low = lax.broadcasted_iota(jnp.int32, (128, 128), 1) < 64

    def half(block, side):
        tile = scr[:, pl.ds(pl.multiple_of((block // 2) * 128, 128), 128)]
        return jnp.where(block % 2 == side, tile, pltpu.roll(tile, 64, axis=1))

    for j in range(16):
        out_ref[:, j * 128 : (j + 1) * 128] = jnp.where(
            low, half(inverse[2 * j], 0), half(inverse[2 * j + 1], 1)
        ).astype(BF16)


def prep(owner, x, gain):
    return pl.pallas_call(
        prep_kernel,
        out_shape=jax.ShapeDtypeStruct(x.shape, BF16),
        in_specs=[
            pl.BlockSpec(memory_space=pltpu.SMEM),
            pl.BlockSpec(memory_space=pltpu.VMEM),
            pl.BlockSpec(memory_space=pltpu.VMEM),
        ],
        out_specs=pl.BlockSpec(memory_space=pltpu.VMEM),
        scratch_shapes=[pltpu.VMEM(x.shape, F32), pltpu.SMEM((32,), jnp.int32)],
        name="prep",
    )(owner, x, gain)


def finish_kernel(owner_ref, live_ref, x_ref, out_ref, scr):
    scr[...] = x_ref[...].astype(F32)
    live = lax.broadcasted_iota(jnp.int32, (128, 128), 0) < live_ref[0]
    low = lax.broadcasted_iota(jnp.int32, (128, 128), 1) < 64

    def half(block, side):
        tile = scr[:, pl.ds(pl.multiple_of((block // 2) * 128, 128), 128)]
        return jnp.where(block % 2 == side, tile, pltpu.roll(tile, 64, axis=1))

    for j in range(16):
        tile = jnp.where(low, half(owner_ref[2 * j], 0), half(owner_ref[2 * j + 1], 1))
        out_ref[:, j * 128 : (j + 1) * 128] = jnp.where(live, tile, 0.0).astype(BF16)


def finish(owner, live, x):
    return pl.pallas_call(
        finish_kernel,
        out_shape=jax.ShapeDtypeStruct(x.shape, BF16),
        in_specs=[
            pl.BlockSpec(memory_space=pltpu.SMEM),
            pl.BlockSpec(memory_space=pltpu.SMEM),
            pl.BlockSpec(memory_space=pltpu.VMEM),
        ],
        out_specs=pl.BlockSpec(memory_space=pltpu.VMEM),
        scratch_shapes=[pltpu.VMEM(x.shape, F32)],
        name="finish",
    )(owner, live, x)


def body(
    prompt_states,
    lengths,
    bucket_owner,
    w_in,
    w_gates,
    out_weight,
    conv_weight,
    decay_rate,
    dt_bias,
    in_gain,
    head_gain,
):
    tok_rows = prompt_states.shape[1]
    rows = w_in.shape[0]
    normed = prep(bucket_owner, prompt_states[0], in_gain[None, :])
    packed = jnp.concatenate(
        [
            w_in.reshape(rows, -1),
            jnp.pad(w_gates.reshape(rows, -1), ((0, 0), (0, 120))),
            out_weight.reshape(rows, -1),
        ],
        axis=1,
    )
    full_rows = lax.all_gather(normed, "tp", axis=0, tiled=True)
    weights = lax.all_gather(packed, "roll", axis=0, tiled=True)
    taps = conv_weight.astype(F32).reshape(4, -1)
    lane_pad = ((0, 0), (0, 124))
    rate = jnp.pad(decay_rate.reshape(1, -1), lane_pad)
    bias = jnp.pad(dt_bias.reshape(1, -1), lane_pad)
    partial = mixer(full_rows, weights, taps, rate, bias, head_gain[None, :])
    mine = lax.psum_scatter(partial, "tp", scatter_dimension=0, tiled=True)
    live = lengths - lax.axis_index("tp") * tok_rows
    return finish(bucket_owner, live, mine)[None]


def solution(mesh):
    in_specs = (
        P("roll", "tp", None),
        P("roll"),
        P(),
        P("roll", None, "tp"),
        P("roll", None, None, "tp"),
        P("roll", None, "tp"),
        P(None, None, "tp"),
        P(None, "tp"),
        P(None, "tp"),
        P(),
        P(),
    )
    out_specs = P("roll", "tp", None)
    return jax.shard_map(body, mesh=mesh, in_specs=in_specs, out_specs=out_specs, check_vma=False)
```

```python
import jax
import jax.numpy as jnp
from jax import lax
from jax.experimental import pallas as pl
from jax.experimental.pallas import tpu as pltpu
from jax.sharding import PartitionSpec as P

CH = 64
NG = 4
ROWS = CH * NG
F32 = jnp.float32
BF16 = jnp.bfloat16
HIGHEST = lax.Precision.HIGHEST


def mm(a, b):
    return jnp.dot(a, b, preferred_element_type=F32)


def mm_nt(a, b):
    return lax.dot_general(a, b, (((1,), (1,)), ((), ())), preferred_element_type=F32)


def mm_tn(a, b):
    return lax.dot_general(a, b, (((0,), (0,)), ((), ())), preferred_element_type=F32)


def mm_exact(a, b):
    return jnp.dot(a, b, preferred_element_type=F32, precision=HIGHEST)


def silu(v):
    return v / (1.0 + jnp.exp(-v))


def mixer_kernel(x_ref, w_ref, taps_ref, rate_ref, bias_ref, gain_ref, out_ref, pscr, oscr, state):
    step = pl.program_id(0)

    @pl.when(step == 0)
    def _():
        pscr[0:8, :] = jnp.zeros((8, 1024), F32)
        state[...] = jnp.zeros_like(state)

    @pl.when(step > 0)
    def _():
        pscr[0:8, :] = pscr[ROWS : ROWS + 8, :]

    x = x_ref[...]
    gates = mm(x, w_ref[:, 1536:1664])
    pscr[8 : 8 + ROWS, :] = mm(x, w_ref[:, 0:1024])

    biased = gates + bias_ref[...]
    soft = jnp.maximum(biased, 0.0) + jnp.log(1.0 + jnp.exp(-jnp.abs(biased)))
    decay = -rate_ref[...] * soft
    beta = 1.0 / (1.0 + jnp.exp(-gates))
    ri = lax.broadcasted_iota(jnp.int32, (ROWS, ROWS), 0)
    ci = lax.broadcasted_iota(jnp.int32, (ROWS, ROWS), 1)
    same = (ri // CH) == (ci // CH)
    tri = jnp.where(same & (ri >= ci), 1.0, 0.0)
    totals = mm_exact(tri, decay)
    lane_r = lax.broadcasted_iota(jnp.int32, (128, 256), 0)
    lane_c = lax.broadcasted_iota(jnp.int32, (128, 256), 1)
    spread = jnp.where(lane_r == lane_c // CH, 1.0, 0.0)
    spread_b = jnp.where(lane_r == lane_c // CH + 4, 1.0, 0.0)
    lane_r5 = lax.broadcasted_iota(jnp.int32, (128, 512), 0)
    lane_c5 = lax.broadcasted_iota(jnp.int32, (128, 512), 1)
    spread5 = jnp.where(lane_r5 == lane_c5 // 128, 1.0, 0.0)
    spread5_b = jnp.where(lane_r5 == lane_c5 // 128 + 4, 1.0, 0.0)
    tot_w = mm_exact(totals, spread)
    beta_w = mm_exact(beta, spread_b)
    tot_v = mm_exact(totals, spread5)
    beta_v = mm_exact(beta, spread5_b)
    grow_v = jnp.exp(tot_v)

    mixed = []
    for c in range(4):
        acc = None
        for i in range(4):
            term = taps_ref[i : i + 1, c * 256 : (c + 1) * 256] * pscr[8 - i : 8 - i + ROWS, c * 256 : (c + 1) * 256]
            acc = term if acc is None else acc + term
        mixed.append(silu(acc))

    def unit(v):
        parts = []
        for h in range(2):
            p = v[:, h * 128 : (h + 1) * 128]
            parts.append(p * lax.rsqrt(jnp.sum(p * p, axis=-1, keepdims=True) + 1e-6))
        return jnp.concatenate(parts, axis=1)

    query = (unit(mixed[0]) * (128.0 ** -0.5)).astype(BF16)
    keys_f = unit(mixed[1])
    keys = keys_f.astype(BF16)

    wi = lax.broadcasted_iota(jnp.int32, (CH, 256), 0)
    wj = lax.broadcasted_iota(jnp.int32, (CH, 256), 1) % CH
    eye = wi == wj
    lower = wi >= wj
    strict = wi > wj
    bd_mask = same
    kmask = (lax.broadcasted_iota(jnp.int32, (128, 256), 0) // CH) == (
        lax.broadcasted_iota(jnp.int32, (128, 256), 1) // 128
    )

    def bd(v):
        vb = v.astype(BF16)
        return jnp.where(bd_mask, jnp.concatenate([vb] * 4, axis=0), jnp.zeros((), BF16))

    chunks = range(NG)
    rows = [slice(c * CH, (c + 1) * CH) for c in chunks]
    sys_w, score_w = [], []
    for c in chunks:
        k_c, q_c = keys[rows[c]], query[rows[c]]
        k_bd = jnp.where(kmask, jnp.concatenate([k_c, k_c], axis=0), jnp.zeros((), BF16))
        both = mm_nt(jnp.concatenate([k_c, q_c], axis=0), k_bd)
        kk = jnp.concatenate([both[:CH], both[:CH]], axis=1)
        qk = jnp.concatenate([both[CH:], both[CH:]], axis=1)
        t_c = tot_w[rows[c]]
        t_row = jnp.sum(jnp.where(eye, t_c, 0.0), axis=0, keepdims=True)
        inside = jnp.where(lower, jnp.exp(jnp.where(lower, t_c - t_row, 0.0)), 0.0)
        sys_w.append(jnp.where(strict, beta_w[rows[c]] * kk * inside, 0.0))
        score_w.append(qk * inside)

    eye_f = jnp.where(eye, 1.0, 0.0)

    def block(n):
        return (wi // n) == (wj // n)

    base = [jnp.where(block(8), a, 0.0) for a in sys_w]
    base2 = [mm(d.astype(BF16), bd(d)) for d in base]
    base4 = [mm(d.astype(BF16), bd(d)) for d in base2]
    inv = [eye_f - d for d in base]
    inv = [t + mm(t.astype(BF16), bd(d)) for t, d in zip(inv, base2)]
    inv = [t + mm(t.astype(BF16), bd(d)) for t, d in zip(inv, base4)]
    for n in (16, 32, 64):
        pick = block(n) & jnp.logical_not(block(n // 2))
        low = [jnp.where(pick, a, 0.0).astype(BF16) for a in sys_w]
        mid = [mm(l, bd(t)) for l, t in zip(low, inv)]
        inv = [t - mm(t.astype(BF16), bd(m)) for t, m in zip(inv, mid)]
    fixed = []
    for c in chunks:
        a_hi = sys_w[c].astype(BF16)
        a_lo = (sys_w[c] - a_hi.astype(F32)).astype(BF16)
        t_hi = inv[c].astype(BF16)
        t_lo = (inv[c] - t_hi.astype(F32)).astype(BF16)
        both = mm(jnp.concatenate([a_hi, a_lo], axis=0), bd(t_hi))
        prod = both[:CH] + both[CH:] + mm(a_hi, bd(t_lo))
        resid = eye_f - inv[c] - prod
        fixed.append(inv[c] + mm(t_hi, bd(resid)))
    inv = fixed

    solved = []
    for c in chunks:
        parts = []
        for s in range(2):
            for h in range(2):
                n = s * 2 + h
                b = beta_v[rows[c], n * 128 : (n + 1) * 128]
                g = grow_v[rows[c], n * 128 : (n + 1) * 128]
                v = mixed[2 + s][rows[c], h * 128 : (h + 1) * 128]
                k = keys_f[rows[c], h * 128 : (h + 1) * 128]
                parts.append(jnp.concatenate([(b * v).astype(BF16), (b * g * k).astype(BF16)], axis=1))
        rhs = jnp.concatenate(parts, axis=0)
        solved.append(mm(bd(inv[c]), rhs))
    score_bd = [bd(s) for s in score_w]

    for c in chunks:
        reads = []
        for h in range(2):
            lhs = jnp.concatenate(
                [
                    solved[c][h * CH : (h + 1) * CH, 128:256].astype(BF16),
                    solved[c][(2 + h) * CH : (3 + h) * CH, 128:256].astype(BF16),
                    query[rows[c], h * 128 : (h + 1) * 128],
                ],
                axis=0,
            )
            reads.append(mm(lhs, state[h].astype(BF16)))
        updates, writes = [None] * 4, [None] * 4
        last = tot_v[(c + 1) * CH - 1 : (c + 1) * CH, :]
        for s in range(2):
            for h in range(2):
                n = s * 2 + h
                u = solved[c][n * CH : (n + 1) * CH, 0:128] - reads[h][s * CH : (s + 1) * CH, s * 128 : (s + 1) * 128]
                carry = jnp.exp(last[:, n * 128 : (n + 1) * 128] - tot_v[rows[c], n * 128 : (n + 1) * 128])
                updates[n] = u.astype(BF16)
                writes[n] = (carry * u).astype(BF16)
        for h in range(2):
            decay_all = jnp.concatenate(
                [jnp.exp(last[:, h * 128 : (h + 1) * 128]), jnp.exp(last[:, (2 + h) * 128 : (3 + h) * 128])], axis=1
            )
            write = jnp.concatenate([writes[h], writes[2 + h]], axis=1)
            state[h] = decay_all * state[h] + mm_tn(keys[rows[c], h * 128 : (h + 1) * 128], write)
        inner = mm(score_bd[c], jnp.concatenate(updates, axis=0))
        for s in range(2):
            for h in range(2):
                n = s * 2 + h
                oscr[rows[c], n * 128 : (n + 1) * 128] = (
                    grow_v[rows[c], n * 128 : (n + 1) * 128] * reads[h][2 * CH :, s * 128 : (s + 1) * 128]
                    + inner[n * CH : (n + 1) * CH]
                )

    og = mm(x, w_ref[:, 1024:1536])
    hidden = []
    for n in range(4):
        r = oscr[:, n * 128 : (n + 1) * 128]
        r = r * lax.rsqrt(jnp.mean(r * r, axis=-1, keepdims=True) + 1e-6) * gain_ref[...]
        hidden.append((r * silu(og[:, n * 128 : (n + 1) * 128])).astype(BF16))
    hidden = jnp.concatenate(hidden, axis=1)
    out_ref[...] = mm_nt(hidden, w_ref[:, 1664:2176]).astype(BF16)


def mixer(x, w, taps, rate, bias, gain):
    seq = x.shape[0]
    return pl.pallas_call(
        mixer_kernel,
        grid=(seq // ROWS,),
        out_shape=jax.ShapeDtypeStruct((seq, 2048), BF16),
        in_specs=[
            pl.BlockSpec((ROWS, 2048), lambda i: (i, 0)),
            pl.BlockSpec((2048, 2176), lambda i: (0, 0), pipeline_mode=pl.Buffered(1)),
            pl.BlockSpec((4, 1024), lambda i: (0, 0)),
            pl.BlockSpec((1, 128), lambda i: (0, 0)),
            pl.BlockSpec((1, 128), lambda i: (0, 0)),
            pl.BlockSpec((1, 128), lambda i: (0, 0)),
        ],
        out_specs=pl.BlockSpec((ROWS, 2048), lambda i: (i, 0)),
        scratch_shapes=[
            pltpu.VMEM((ROWS + 8, 1024), F32),
            pltpu.VMEM((ROWS, 512), F32),
            pltpu.VMEM((2, 128, 256), F32),
        ],
        compiler_params=pltpu.CompilerParams(vmem_limit_bytes=48 << 20),
        name="mixer",
    )(x, w, taps, rate, bias, gain)


def prep_kernel(owner_ref, x_ref, gain_ref, out_ref, scr, inverse):
    x = x_ref[...].astype(F32)
    scale = lax.rsqrt(jnp.mean(x * x, axis=-1, keepdims=True) + 1e-6)
    scr[...] = x * scale * gain_ref[...]
    for b in range(32):
        inverse[owner_ref[b]] = b
    low = lax.broadcasted_iota(jnp.int32, (128, 128), 1) < 64

    def half(block, side):
        tile = scr[:, pl.ds(pl.multiple_of((block // 2) * 128, 128), 128)]
        return jnp.where(block % 2 == side, tile, pltpu.roll(tile, 64, axis=1))

    for j in range(16):
        out_ref[:, j * 128 : (j + 1) * 128] = jnp.where(
            low, half(inverse[2 * j], 0), half(inverse[2 * j + 1], 1)
        ).astype(BF16)


def prep(owner, x, gain):
    return pl.pallas_call(
        prep_kernel,
        out_shape=jax.ShapeDtypeStruct(x.shape, BF16),
        in_specs=[
            pl.BlockSpec(memory_space=pltpu.SMEM),
            pl.BlockSpec(memory_space=pltpu.VMEM),
            pl.BlockSpec(memory_space=pltpu.VMEM),
        ],
        out_specs=pl.BlockSpec(memory_space=pltpu.VMEM),
        scratch_shapes=[pltpu.VMEM(x.shape, F32), pltpu.SMEM((32,), jnp.int32)],
        name="prep",
    )(owner, x, gain)


def finish_kernel(owner_ref, live_ref, x_ref, out_ref, scr):
    scr[...] = x_ref[...].astype(F32)
    live = lax.broadcasted_iota(jnp.int32, (128, 128), 0) < live_ref[0]
    low = lax.broadcasted_iota(jnp.int32, (128, 128), 1) < 64

    def half(block, side):
        tile = scr[:, pl.ds(pl.multiple_of((block // 2) * 128, 128), 128)]
        return jnp.where(block % 2 == side, tile, pltpu.roll(tile, 64, axis=1))

    for j in range(16):
        tile = jnp.where(low, half(owner_ref[2 * j], 0), half(owner_ref[2 * j + 1], 1))
        out_ref[:, j * 128 : (j + 1) * 128] = jnp.where(live, tile, 0.0).astype(BF16)


def finish(owner, live, x):
    return pl.pallas_call(
        finish_kernel,
        out_shape=jax.ShapeDtypeStruct(x.shape, BF16),
        in_specs=[
            pl.BlockSpec(memory_space=pltpu.SMEM),
            pl.BlockSpec(memory_space=pltpu.SMEM),
            pl.BlockSpec(memory_space=pltpu.VMEM),
        ],
        out_specs=pl.BlockSpec(memory_space=pltpu.VMEM),
        scratch_shapes=[pltpu.VMEM(x.shape, F32)],
        name="finish",
    )(owner, live, x)


MESH = pl.DeviceIdType.MESH


class Place:
    def __init__(self):
        roll, tp = lax.axis_index("roll"), lax.axis_index("tp")
        self.zl, self.x, self.core = roll // 8, (roll // 2) % 4, roll % 2
        self.zh, self.y = tp // 4, tp % 4

    def at(self, zl=None, x=None, core=None, zh=None, y=None):
        zl = self.zl if zl is None else zl
        x = self.x if x is None else x
        core = self.core if core is None else core
        zh = self.zh if zh is None else zh
        y = self.y if y is None else y
        return (zl * 8 + x * 2 + core, zh * 4 + y)

    def along_z(self, hops):
        z = (self.zh * 4 + self.zl + hops) % 8
        return self.at(zl=z % 4, zh=z // 4)


def meet(devices):
    barrier = pltpu.get_barrier_semaphore()
    for device in devices:
        pl.semaphore_signal(barrier, inc=1, device_id=device, device_id_type=MESH)
    pl.semaphore_wait(barrier, len(devices))


def gather_kernel(x_ref, w_ref, xo, wo, transit, zs_up, zs_dn, zr, ws, wr, ys, yr, own_sem):
    me = Place()
    left_x, right_x = me.at(x=(me.x + 3) % 4), me.at(x=(me.x + 1) % 4)
    left_y, right_y = me.at(y=(me.y + 3) % 4), me.at(y=(me.y + 1) % 4)
    up, down = me.at(zl=(me.zl + 1) % 4), me.at(zl=(me.zl + 3) % 4)
    sibling, partner = me.at(core=1 - me.core), me.at(zh=1 - me.zh)
    behind, ahead = me.along_z(6), me.along_z(2)
    meet([left_x, right_x, left_y, right_y, up, down, sibling, partner, behind, ahead])

    def copy(src, dst, send, recv, device):
        return pltpu.make_async_remote_copy(
            src_ref=src, dst_ref=dst, send_sem=send, recv_sem=recv, device_id=device, device_id_type=MESH
        )

    sent = []

    def send(src, dst, sems, i, device):
        c = copy(src, dst, sems[0].at[i], sems[1].at[i], device)
        c.start()
        sent.append(c)

    def arrived(dst, sems, i):
        copy(dst, dst, sems[0].at[i], sems[1].at[i], sibling).wait_recv()

    W, Y = (ws, wr), (ys, yr)

    def shard(zl, x, core):
        return wo.at[pl.ds(pl.multiple_of((zl * 8 + x * 2 + core) * 64, 64), 64)]

    def part(zl, x, core, p):
        return wo.at[pl.ds(pl.multiple_of((zl * 8 + x * 2 + core) * 64 + p * 32, 32), 32)]

    def block(zh, y, p):
        return xo.at[pl.ds(pl.multiple_of((zh * 4 + y) * 128 + p * 64, 64), 64)]

    order = [[0, 1, 2, 3], [1, 0, 2, 3], [2, 1, 3, 0], [3, 2, 1, 0]]
    slot = [
        jnp.where(me.zl == 0, order[0][j], jnp.where(me.zl == 1, order[1][j], jnp.where(me.zl == 2, order[2][j], order[3][j])))
        for j in range(4)
    ]
    xl, xr = (me.x + 3) % 4, (me.x + 1) % 4
    xf = (me.x + 2) % 4
    yl, yr_, yf = (me.y + 3) % 4, (me.y + 1) % 4, (me.y + 2) % 4
    mine_x = [x_ref.at[pl.ds(p * 64, 64)] for p in range(2)]

    def z_up(src, z):
        return copy(src, shard(z, me.x, me.core), zs_up.at[z], zr.at[z], up)

    def z_down(src, z):
        return copy(src, shard(z, me.x, me.core), zs_dn.at[z], zr.at[z], down)

    def spread_x(src, j):
        z = slot[j]
        for i, device in ((0, right_x), (1, left_x)):
            send(src, shard(z, me.x, me.core), W, j * 8 + i, device)
        send(src, shard(z, me.x, me.core), W, j * 8 + 4, sibling)

    def relay_x(j):
        z = slot[j]
        arrived(shard(z, xl, me.core), W, j * 8)
        send(part(z, xl, me.core, 0), part(z, xl, me.core, 0), W, j * 8 + 2, right_x)
        arrived(shard(z, xr, me.core), W, j * 8 + 1)
        send(part(z, xr, me.core, 1), part(z, xr, me.core, 1), W, j * 8 + 3, left_x)
        send(shard(z, xl, me.core), shard(z, xl, me.core), W, j * 8 + 5, sibling)
        send(shard(z, xr, me.core), shard(z, xr, me.core), W, j * 8 + 6, sibling)

    def far_x(j):
        z = slot[j]
        arrived(part(z, xf, me.core, 0), W, j * 8 + 2)
        arrived(part(z, xf, me.core, 1), W, j * 8 + 3)
        send(shard(z, xf, me.core), shard(z, xf, me.core), W, j * 8 + 7, sibling)

    def take_z(j):
        z = slot[j]
        copy(shard(z, me.x, me.core), shard(z, me.x, me.core), zs_up.at[z], zr.at[z], up).wait_recv()

        @pl.when((z < me.zl) & (me.zl < 3))
        def _():
            z_up(shard(z, me.x, me.core), z).start()

        @pl.when((z > me.zl) & (me.zl > 0))
        def _():
            z_down(shard(z, me.x, me.core), z).start()

        spread_x(shard(z, me.x, me.core), j)

    def spread_y(src, zh, b, p):
        send(src, block(zh, me.y, p), Y, b * 6 + p, right_y)
        send(src, block(zh, me.y, p), Y, b * 6 + 2 + p, left_y)

    def relay_y(zh, b):
        arrived(block(zh, yl, 0), Y, b * 6)
        send(block(zh, yl, 0), block(zh, yl, 0), Y, b * 6 + 4, right_y)
        arrived(block(zh, yr_, 1), Y, b * 6 + 3)
        send(block(zh, yr_, 1), block(zh, yr_, 1), Y, b * 6 + 5, left_y)

    def rest_y(zh, b):
        arrived(block(zh, yl, 1), Y, b * 6 + 1)
        arrived(block(zh, yr_, 0), Y, b * 6 + 2)
        arrived(block(zh, yf, 0), Y, b * 6 + 4)
        arrived(block(zh, yf, 1), Y, b * 6 + 5)

    other = 1 - me.zh
    send(mine_x[1], transit, Y, 13, behind)
    send(mine_x[0], block(me.zh, me.y, 0), Y, 12, partner)

    @pl.when(me.zl < 3)
    def _():
        z_up(w_ref, me.zl).start()

    @pl.when(me.zl > 0)
    def _():
        z_down(w_ref, me.zl).start()

    spread_x(w_ref, 0)
    spread_y(mine_x[0], me.zh, 0, 0)
    spread_y(mine_x[1], me.zh, 0, 1)
    keep_w = pltpu.make_async_copy(w_ref, shard(me.zl, me.x, me.core), own_sem.at[0])
    keep_w.start()
    keep_x = pltpu.make_async_copy(x_ref, xo.at[pl.ds(pl.multiple_of((me.zh * 4 + me.y) * 128, 128), 128)], own_sem.at[1])
    keep_x.start()

    relay_x(0)
    take_z(1)
    relay_y(me.zh, 0)
    arrived(transit, Y, 13)
    send(transit, block_of_ahead(me, xo), Y, 14, behind)
    relay_x(1)
    far_x(0)
    take_z(2)
    arrived(block(other, me.y, 0), Y, 12)
    spread_y(block(other, me.y, 0), other, 1, 0)
    relay_x(2)
    far_x(1)
    take_z(3)
    arrived(block(other, me.y, 1), Y, 14)
    spread_y(block(other, me.y, 1), other, 1, 1)
    relay_x(3)
    far_x(2)
    relay_y(other, 1)
    far_x(3)
    rest_y(me.zh, 0)
    rest_y(other, 1)
    for j in range(4):
        z = slot[j]
        for i, x in ((4, me.x), (5, xl), (6, xr), (7, xf)):
            arrived(shard(z, x, 1 - me.core), W, j * 8 + i)
    keep_w.wait()
    keep_x.wait()
    for c in sent:
        c.wait_send()
    for j in range(4):
        z = slot[j]

        @pl.when((z <= me.zl) & (me.zl < 3))
        def _():
            z_up(shard(z, me.x, me.core), z).wait_send()

        @pl.when((z >= me.zl) & (me.zl > 0))
        def _():
            z_down(shard(z, me.x, me.core), z).wait_send()


def block_of_ahead(me, xo):
    z = (me.zh * 4 + me.zl + 2) % 8
    return xo.at[pl.ds(pl.multiple_of(((z // 4) * 4 + me.y) * 128 + 64, 64), 64)]


DMA = pltpu.SemaphoreType.DMA


def gather(rows, packed):
    return pl.pallas_call(
        gather_kernel,
        out_shape=(
            jax.ShapeDtypeStruct((8 * rows.shape[0], rows.shape[1]), BF16),
            jax.ShapeDtypeStruct((32 * packed.shape[0], packed.shape[1]), BF16),
        ),
        in_specs=[pl.BlockSpec(memory_space=pl.ANY)] * 2,
        out_specs=(pl.BlockSpec(memory_space=pl.ANY),) * 2,
        scratch_shapes=[
            pltpu.VMEM((64, 2048), BF16),
            DMA((4,)), DMA((4,)), DMA((4,)),
            DMA((32,)), DMA((32,)),
            DMA((15,)), DMA((15,)),
            DMA((2,)),
        ],
        compiler_params=pltpu.CompilerParams(collective_id=0, has_side_effects=True),
        name="gather",
    )(rows, packed)


def scatter_kernel(p_ref, out_ref, first, full, mixed, summed, landed, transit, ss, rs):
    me = Place()
    left_y, right_y = me.at(y=(me.y + 3) % 4), me.at(y=(me.y + 1) % 4)
    partner, behind, ahead = me.at(zh=1 - me.zh), me.along_z(6), me.along_z(2)
    meet([left_y, right_y, partner, behind, ahead])
    yl, yr_, yf = (me.y + 3) % 4, (me.y + 1) % 4, (me.y + 2) % 4
    sent = []

    def send(src, dst, i, device):
        c = pltpu.make_async_remote_copy(
            src_ref=src, dst_ref=dst, send_sem=ss.at[i], recv_sem=rs.at[i], device_id=device, device_id_type=MESH
        )
        c.start()
        sent.append(c)

    def arrived(dst, i):
        pltpu.make_async_remote_copy(
            src_ref=dst, dst_ref=dst, send_sem=ss.at[i], recv_sem=rs.at[i], device_id=partner, device_id_type=MESH
        ).wait_recv()

    def half(zh, y, p):
        return p_ref.at[pl.ds(pl.multiple_of((zh * 4 + y) * 128 + p * 64, 64), 64)]

    halves = (1 - me.zh, me.zh)
    for b, zh in enumerate(halves):
        send(half(zh, yf, 0), first.at[b, 0], b * 6, right_y)
        send(half(zh, yf, 1), first.at[b, 1], b * 6 + 1, left_y)
        send(half(zh, yr_, 1), full.at[b, 0, 1], b * 6 + 2, right_y)
        send(half(zh, yl, 0), full.at[b, 1, 0], b * 6 + 3, left_y)

    def relay(b, zh):
        arrived(first.at[b, 0], b * 6)
        mixed[b, 0] = (half(zh, yr_, 0)[...].astype(F32) + first[b, 0].astype(F32)).astype(BF16)
        send(mixed.at[b, 0], full.at[b, 0, 0], b * 6 + 4, right_y)
        arrived(first.at[b, 1], b * 6 + 1)
        mixed[b, 1] = (half(zh, yl, 1)[...].astype(F32) + first[b, 1].astype(F32)).astype(BF16)
        send(mixed.at[b, 1], full.at[b, 1, 1], b * 6 + 5, left_y)

    def total(b, zh, p):
        if p == 0:
            arrived(full.at[b, 1, 0], b * 6 + 3)
            arrived(full.at[b, 0, 0], b * 6 + 4)
        else:
            arrived(full.at[b, 0, 1], b * 6 + 2)
            arrived(full.at[b, 1, 1], b * 6 + 5)
        return half(zh, me.y, p)[...].astype(F32) + full[b, 0, p].astype(F32) + full[b, 1, p].astype(F32)

    relay(0, halves[0])
    summed[1] = total(0, halves[0], 1).astype(BF16)
    send(summed.at[1], transit, 12, behind)
    summed[0] = total(0, halves[0], 0).astype(BF16)
    send(summed.at[0], landed.at[0], 13, partner)
    relay(1, halves[1])
    arrived(transit, 12)
    send(transit, landed.at[1], 14, behind)
    for p in range(2):
        t = total(1, halves[1], p)
        arrived(landed.at[p], 13 + p)
        out_ref[p * 64 : (p + 1) * 64, :] = (t + landed[p].astype(F32)).astype(BF16)
    for c in sent:
        c.wait_send()


def scatter(partial):
    width = partial.shape[1]
    return pl.pallas_call(
        scatter_kernel,
        out_shape=jax.ShapeDtypeStruct((partial.shape[0] // 8, width), BF16),
        in_specs=[pl.BlockSpec(memory_space=pltpu.VMEM)],
        out_specs=pl.BlockSpec(memory_space=pltpu.VMEM),
        scratch_shapes=[
            pltpu.VMEM((2, 2, 64, width), BF16),
            pltpu.VMEM((2, 2, 2, 64, width), BF16),
            pltpu.VMEM((2, 2, 64, width), BF16),
            pltpu.VMEM((2, 64, width), BF16),
            pltpu.VMEM((2, 64, width), BF16),
            pltpu.VMEM((64, width), BF16),
            DMA((15,)), DMA((15,)),
        ],
        compiler_params=pltpu.CompilerParams(
            collective_id=1, has_side_effects=True, vmem_limit_bytes=32 << 20
        ),
        name="scatter",
    )(partial)


def body(
    prompt_states,
    lengths,
    bucket_owner,
    w_in,
    w_gates,
    out_weight,
    conv_weight,
    decay_rate,
    dt_bias,
    in_gain,
    head_gain,
):
    tok_rows = prompt_states.shape[1]
    rows = w_in.shape[0]
    normed = prep(bucket_owner, prompt_states[0], in_gain[None, :])
    packed = jnp.concatenate(
        [
            w_in.reshape(rows, -1),
            jnp.pad(w_gates.reshape(rows, -1), ((0, 0), (0, 120))),
            out_weight.reshape(rows, -1),
        ],
        axis=1,
    )
    full_rows, weights = gather(normed, packed)
    taps = conv_weight.astype(F32).reshape(4, -1)
    lane_pad = ((0, 0), (0, 124))
    rate = jnp.pad(decay_rate.reshape(1, -1), lane_pad)
    bias = jnp.pad(dt_bias.reshape(1, -1), lane_pad)
    partial = mixer(full_rows, weights, taps, rate, bias, head_gain[None, :])
    mine = scatter(partial)
    live = lengths - lax.axis_index("tp") * tok_rows
    return finish(bucket_owner, live, mine)[None]


def solution(mesh):
    in_specs = (
        P("roll", "tp", None),
        P("roll"),
        P(),
        P("roll", None, "tp"),
        P("roll", None, None, "tp"),
        P("roll", None, "tp"),
        P(None, None, "tp"),
        P(None, "tp"),
        P(None, "tp"),
        P(),
        P(),
    )
    out_specs = P("roll", "tp", None)
    return jax.shard_map(body, mesh=mesh, in_specs=in_specs, out_specs=out_specs, check_vma=False)
```

```python
import jax
import jax.numpy as jnp
from jax import lax
from jax.experimental import pallas as pl
from jax.experimental.pallas import tpu as pltpu
from jax.sharding import PartitionSpec as P

CH = 64
NG = 4
ROWS = CH * NG
F32 = jnp.float32
BF16 = jnp.bfloat16
HIGHEST = lax.Precision.HIGHEST


def mm(a, b):
    return jnp.dot(a, b, preferred_element_type=F32)


def mm_nt(a, b):
    return lax.dot_general(a, b, (((1,), (1,)), ((), ())), preferred_element_type=F32)


def mm_tn(a, b):
    return lax.dot_general(a, b, (((0,), (0,)), ((), ())), preferred_element_type=F32)


def mm_exact(a, b):
    return jnp.dot(a, b, preferred_element_type=F32, precision=HIGHEST)


def silu(v):
    return v / (1.0 + jnp.exp(-v))


def prep_kernel(owner_ref, x_ref, gain_ref, out_ref, scr, inverse):
    x = x_ref[...].astype(F32)
    scale = lax.rsqrt(jnp.mean(x * x, axis=-1, keepdims=True) + 1e-6)
    scr[...] = x * scale * gain_ref[...]
    for b in range(32):
        inverse[owner_ref[b]] = b
    low = lax.broadcasted_iota(jnp.int32, (128, 128), 1) < 64

    def half(block, side):
        tile = scr[:, pl.ds(pl.multiple_of((block // 2) * 128, 128), 128)]
        return jnp.where(block % 2 == side, tile, pltpu.roll(tile, 64, axis=1))

    for j in range(16):
        out_ref[:, j * 128 : (j + 1) * 128] = jnp.where(
            low, half(inverse[2 * j], 0), half(inverse[2 * j + 1], 1)
        ).astype(BF16)


def prep(owner, x, gain):
    return pl.pallas_call(
        prep_kernel,
        out_shape=jax.ShapeDtypeStruct(x.shape, BF16),
        in_specs=[
            pl.BlockSpec(memory_space=pltpu.SMEM),
            pl.BlockSpec(memory_space=pltpu.VMEM),
            pl.BlockSpec(memory_space=pltpu.VMEM),
        ],
        out_specs=pl.BlockSpec(memory_space=pltpu.VMEM),
        scratch_shapes=[pltpu.VMEM(x.shape, F32), pltpu.SMEM((32,), jnp.int32)],
        name="prep",
    )(owner, x, gain)


def finish_kernel(owner_ref, live_ref, x_ref, out_ref, scr):
    scr[...] = x_ref[...].astype(F32)
    live = lax.broadcasted_iota(jnp.int32, (128, 128), 0) < live_ref[0]
    low = lax.broadcasted_iota(jnp.int32, (128, 128), 1) < 64

    def half(block, side):
        tile = scr[:, pl.ds(pl.multiple_of((block // 2) * 128, 128), 128)]
        return jnp.where(block % 2 == side, tile, pltpu.roll(tile, 64, axis=1))

    for j in range(16):
        tile = jnp.where(low, half(owner_ref[2 * j], 0), half(owner_ref[2 * j + 1], 1))
        out_ref[:, j * 128 : (j + 1) * 128] = jnp.where(live, tile, 0.0).astype(BF16)


def finish(owner, live, x):
    return pl.pallas_call(
        finish_kernel,
        out_shape=jax.ShapeDtypeStruct(x.shape, BF16),
        in_specs=[
            pl.BlockSpec(memory_space=pltpu.SMEM),
            pl.BlockSpec(memory_space=pltpu.SMEM),
            pl.BlockSpec(memory_space=pltpu.VMEM),
        ],
        out_specs=pl.BlockSpec(memory_space=pltpu.VMEM),
        scratch_shapes=[pltpu.VMEM(x.shape, F32)],
        name="finish",
    )(owner, live, x)


MESH = pl.DeviceIdType.MESH


class Place:
    def __init__(self):
        roll, tp = lax.axis_index("roll"), lax.axis_index("tp")
        self.zl, self.x, self.core = roll // 8, (roll // 2) % 4, roll % 2
        self.zh, self.y = tp // 4, tp % 4

    def at(self, zl=None, x=None, core=None, zh=None, y=None):
        zl = self.zl if zl is None else zl
        x = self.x if x is None else x
        core = self.core if core is None else core
        zh = self.zh if zh is None else zh
        y = self.y if y is None else y
        return (zl * 8 + x * 2 + core, zh * 4 + y)

    def along_z(self, hops):
        z = (self.zh * 4 + self.zl + hops) % 8
        return self.at(zl=z % 4, zh=z // 4)


def meet(devices):
    barrier = pltpu.get_barrier_semaphore()
    for device in devices:
        pl.semaphore_signal(barrier, inc=1, device_id=device, device_id_type=MESH)
    pl.semaphore_wait(barrier, len(devices))


def gather_kernel(x_ref, w_ref, xo, wo, transit, zs_up, zs_dn, zr, ws, wr, ys, yr, own_sem):
    me = Place()
    left_x, right_x = me.at(x=(me.x + 3) % 4), me.at(x=(me.x + 1) % 4)
    left_y, right_y = me.at(y=(me.y + 3) % 4), me.at(y=(me.y + 1) % 4)
    up, down = me.at(zl=(me.zl + 1) % 4), me.at(zl=(me.zl + 3) % 4)
    sibling, partner = me.at(core=1 - me.core), me.at(zh=1 - me.zh)
    behind, ahead = me.along_z(6), me.along_z(2)
    outer = (me.zh * 4 + me.zl + 2) % 8 < 4
    meet([left_x, right_x, left_y, right_y, up, down, sibling, partner, behind, ahead])

    def copy(src, dst, send, recv, device):
        return pltpu.make_async_remote_copy(
            src_ref=src, dst_ref=dst, send_sem=send, recv_sem=recv, device_id=device, device_id_type=MESH
        )

    sent = []

    def send(src, dst, sems, i, device):
        c = copy(src, dst, sems[0].at[i], sems[1].at[i], device)
        c.start()
        sent.append(c)

    def arrived(dst, sems, i):
        copy(dst, dst, sems[0].at[i], sems[1].at[i], sibling).wait_recv()

    W, Y = (ws, wr), (ys, yr)

    def shard(zl, x, core):
        return wo.at[pl.ds(pl.multiple_of((zl * 8 + x * 2 + core) * 64, 64), 64)]

    def part(zl, x, core, p):
        return wo.at[pl.ds(pl.multiple_of((zl * 8 + x * 2 + core) * 64 + p * 32, 32), 32)]

    def block(zh, y, p):
        return xo.at[pl.ds(pl.multiple_of((zh * 4 + y) * 128 + p * 64, 64), 64)]

    order = [[0, 1, 2, 3], [1, 2, 0, 3], [2, 1, 3, 0], [3, 2, 1, 0]]
    slot = [
        jnp.where(me.zl == 0, order[0][j], jnp.where(me.zl == 1, order[1][j], jnp.where(me.zl == 2, order[2][j], order[3][j])))
        for j in range(4)
    ]
    xl, xr = (me.x + 3) % 4, (me.x + 1) % 4
    xf = (me.x + 2) % 4
    yl, yr_, yf = (me.y + 3) % 4, (me.y + 1) % 4, (me.y + 2) % 4
    mine_x = [x_ref.at[pl.ds(p * 64, 64)] for p in range(2)]

    def z_up(src, z):
        return copy(src, shard(z, me.x, me.core), zs_up.at[z], zr.at[z], up)

    def z_down(src, z):
        return copy(src, shard(z, me.x, me.core), zs_dn.at[z], zr.at[z], down)

    def spread_x(src, j):
        z = slot[j]
        for i, device in ((0, right_x), (1, left_x)):
            send(src, shard(z, me.x, me.core), W, j * 8 + i, device)
        send(src, shard(z, me.x, me.core), W, j * 8 + 4, sibling)

    def relay_x(j):
        z = slot[j]
        arrived(shard(z, xl, me.core), W, j * 8)
        send(part(z, xl, me.core, 0), part(z, xl, me.core, 0), W, j * 8 + 2, right_x)
        arrived(shard(z, xr, me.core), W, j * 8 + 1)
        send(part(z, xr, me.core, 1), part(z, xr, me.core, 1), W, j * 8 + 3, left_x)
        send(shard(z, xl, me.core), shard(z, xl, me.core), W, j * 8 + 5, sibling)
        send(shard(z, xr, me.core), shard(z, xr, me.core), W, j * 8 + 6, sibling)

    def far_x(j):
        z = slot[j]
        arrived(part(z, xf, me.core, 0), W, j * 8 + 2)
        arrived(part(z, xf, me.core, 1), W, j * 8 + 3)
        send(shard(z, xf, me.core), shard(z, xf, me.core), W, j * 8 + 7, sibling)

    def take_z(j):
        z = slot[j]
        copy(shard(z, me.x, me.core), shard(z, me.x, me.core), zs_up.at[z], zr.at[z], up).wait_recv()

        @pl.when((z < me.zl) & (me.zl < 3))
        def _():
            z_up(shard(z, me.x, me.core), z).start()

        @pl.when((z > me.zl) & (me.zl > 0))
        def _():
            z_down(shard(z, me.x, me.core), z).start()

        spread_x(shard(z, me.x, me.core), j)

    def spread_y(src, zh, b, p):
        send(src, block(zh, me.y, p), Y, b * 6 + p, right_y)
        send(src, block(zh, me.y, p), Y, b * 6 + 2 + p, left_y)

    def relay_y(zh, b):
        arrived(block(zh, yl, 0), Y, b * 6)
        send(block(zh, yl, 0), block(zh, yl, 0), Y, b * 6 + 4, right_y)
        arrived(block(zh, yr_, 1), Y, b * 6 + 3)
        send(block(zh, yr_, 1), block(zh, yr_, 1), Y, b * 6 + 5, left_y)

    def rest_y(zh, b):
        arrived(block(zh, yl, 1), Y, b * 6 + 1)
        arrived(block(zh, yr_, 0), Y, b * 6 + 2)
        arrived(block(zh, yf, 0), Y, b * 6 + 4)
        arrived(block(zh, yf, 1), Y, b * 6 + 5)

    other = 1 - me.zh

    def away():
        i = 13 + 2 * me.zh
        return copy(mine_x[1], transit.at[me.zh], ys.at[i], yr.at[i], me.along_z(jnp.where(me.zh == 0, 6, 2)))

    def onward(s):
        i = 14 + 2 * s
        return copy(transit.at[s], block(s, me.y, 1), ys.at[i], yr.at[i], ahead if s else behind)


    @pl.when(me.zl < 3)
    def _():
        z_up(w_ref, me.zl).start()

    @pl.when(me.zl > 0)
    def _():
        z_down(w_ref, me.zl).start()

    spread_x(w_ref, 0)
    away().start()
    send(mine_x[0], block(me.zh, me.y, 0), Y, 12, partner)
    spread_y(mine_x[0], me.zh, 0, 0)
    spread_y(mine_x[1], me.zh, 0, 1)
    keep_w = pltpu.make_async_copy(w_ref, shard(me.zl, me.x, me.core), own_sem.at[0])
    keep_w.start()
    keep_x = pltpu.make_async_copy(x_ref, xo.at[pl.ds(pl.multiple_of((me.zh * 4 + me.y) * 128, 128), 128)], own_sem.at[1])
    keep_x.start()

    take_z(1)
    relay_x(0)
    take_z(2)
    relay_y(me.zh, 0)

    @pl.when(outer)
    def _():
        for s in range(2):
            arrived(transit.at[s], Y, 13 + 2 * s)
            onward(s).start()

    relay_x(1)
    take_z(3)
    far_x(0)
    relay_x(2)
    arrived(block(other, me.y, 0), Y, 12)
    spread_y(block(other, me.y, 0), other, 1, 0)
    far_x(1)
    arrived(block(other, me.y, 1), Y, 14 + 2 * other)
    spread_y(block(other, me.y, 1), other, 1, 1)
    relay_x(3)
    far_x(2)
    relay_y(other, 1)
    far_x(3)
    rest_y(me.zh, 0)
    rest_y(other, 1)
    for j in range(4):
        z = slot[j]
        for i, x in ((4, me.x), (5, xl), (6, xr), (7, xf)):
            arrived(shard(z, x, 1 - me.core), W, j * 8 + i)
    keep_w.wait()
    keep_x.wait()
    for c in sent:
        c.wait_send()
    away().wait_send()

    @pl.when(outer)
    def _():
        for s in range(2):
            onward(s).wait_send()

    for j in range(4):
        z = slot[j]

        @pl.when((z <= me.zl) & (me.zl < 3))
        def _():
            z_up(shard(z, me.x, me.core), z).wait_send()

        @pl.when((z >= me.zl) & (me.zl > 0))
        def _():
            z_down(shard(z, me.x, me.core), z).wait_send()


DMA = pltpu.SemaphoreType.DMA


def gather(rows, packed):
    return pl.pallas_call(
        gather_kernel,
        out_shape=(
            jax.ShapeDtypeStruct((8 * rows.shape[0], rows.shape[1]), BF16),
            jax.ShapeDtypeStruct((32 * packed.shape[0], packed.shape[1]), BF16),
        ),
        in_specs=[pl.BlockSpec(memory_space=pl.ANY)] * 2,
        out_specs=(pl.BlockSpec(memory_space=pl.ANY),) * 2,
        scratch_shapes=[
            pltpu.VMEM((2, 64, 2048), BF16),
            DMA((4,)), DMA((4,)), DMA((4,)),
            DMA((32,)), DMA((32,)),
            DMA((17,)), DMA((17,)),
            DMA((2,)),
        ],
        compiler_params=pltpu.CompilerParams(collective_id=0, has_side_effects=True),
        name="gather",
    )(rows, packed)


class Sums:
    def __init__(self, p_ref, first, full, mixed, kept, summed, landed, transit, ss, rs):
        self.p, self.first, self.full, self.mixed = p_ref, first, full, mixed
        self.kept, self.summed, self.landed, self.transit = kept, summed, landed, transit
        self.ss, self.rs = ss, rs
        me = self.me = Place()
        self.left, self.right = me.at(y=(me.y + 3) % 4), me.at(y=(me.y + 1) % 4)
        self.partner, self.behind, self.ahead = me.at(zh=1 - me.zh), me.along_z(6), me.along_z(2)
        self.outer = (me.zh * 4 + me.zl + 2) % 8 < 4

    def meet(self):
        meet([self.left, self.right, self.partner, self.behind, self.ahead])

    def copy(self, i, src, dst, device):
        return pltpu.make_async_remote_copy(
            src_ref=src, dst_ref=dst, send_sem=self.ss.at[i], recv_sem=self.rs.at[i], device_id=device, device_id_type=MESH
        )

    def half(self, b, y, p):
        return self.p.at[pl.ds(pl.multiple_of((b * 4 + y) * 128 + p * 64, 64), 64)]

    def message(self, b, k):
        y, first, full = self.me.y, self.first, self.full
        far, right, left = (y + 2) % 4, (y + 1) % 4, (y + 3) % 4
        src, dst = (
            (self.half(b, far, 0), first.at[b, 0]),
            (self.half(b, far, 1), first.at[b, 1]),
            (self.half(b, right, 1), full.at[b, 0, 1]),
            (self.half(b, left, 0), full.at[b, 1, 0]),
            (self.mixed.at[b, 0], full.at[b, 0, 0]),
            (self.mixed.at[b, 1], full.at[b, 1, 1]),
        )[k]
        return self.copy(b * 6 + k, src, dst, self.left if k % 2 else self.right)

    def begin(self, b):
        for k in range(4):
            self.message(b, k).start()

    def relay(self, b):
        y = self.me.y
        for p, near in ((0, (y + 1) % 4), (1, (y + 3) % 4)):
            self.message(b, p).wait_recv()
            self.mixed[b, p] = (self.half(b, near, p)[...].astype(F32) + self.first[b, p].astype(F32)).astype(BF16)
            self.message(b, 4 + p).start()

    def across(self, b, p):
        if p == 0:
            return self.copy(12, self.summed.at[0], self.landed.at[0], self.partner)
        return self.copy(13 + 2 * b, self.summed.at[1], self.transit.at[b], self.behind if b else self.ahead)

    def passing(self, b):
        return self.copy(14 + 2 * b, self.transit.at[b], self.landed.at[1], self.behind if b else self.ahead)

    def total(self, b):
        for p in (1, 0):
            for k in ((3, 4), (2, 5))[p]:
                self.message(b, k).wait_recv()
            value = (
                self.half(b, self.me.y, p)[...].astype(F32)
                + self.full[b, 0, p].astype(F32)
                + self.full[b, 1, p].astype(F32)
            )

            @pl.when(self.me.zh == b)
            def _():
                self.kept[p] = value

            @pl.when(self.me.zh != b)
            def _():
                self.summed[p] = value.astype(BF16)
                self.across(b, p).start()

    def pass_on(self, b):
        @pl.when(self.outer)
        def _():
            self.across(b, 1).wait_recv()
            self.passing(b).start()

    def finish(self, out_ref):
        self.across(0, 0).wait_recv()
        for b in range(2):

            @pl.when(self.me.zh == b)
            def _():
                self.passing(b).wait_recv()

        for p in range(2):
            out_ref[p * 64 : (p + 1) * 64, :] = (self.kept[p] + self.landed[p].astype(F32)).astype(BF16)
        for b in range(2):
            for k in range(6):
                self.message(b, k).wait_send()
        self.across(0, 0).wait_send()
        for b in range(2):

            @pl.when(self.me.zh != b)
            def _():
                self.across(b, 1).wait_send()

            @pl.when(self.outer)
            def _():
                self.passing(b).wait_send()


def mixer_kernel(
    x_ref, w_ref, taps_ref, rate_ref, bias_ref, gain_ref, out_ref,
    pscr, oscr, state, p_ref, first, full, mixed, kept, summed, landed, transit, ss, rs,
):
    step = pl.program_id(0)
    across = Sums(p_ref, first, full, mixed, kept, summed, landed, transit, ss, rs)

    @pl.when(step == 0)
    def _():
        across.meet()

    @pl.when(step == 2)
    def _():
        across.begin(0)


    @pl.when(step == 0)
    def _():
        pscr[0:8, :] = jnp.zeros((8, 1024), F32)
        state[...] = jnp.zeros_like(state)

    @pl.when(step > 0)
    def _():
        pscr[0:8, :] = pscr[ROWS : ROWS + 8, :]

    x = x_ref[...]
    gates = mm(x, w_ref[:, 1536:1664])
    pscr[8 : 8 + ROWS, :] = mm(x, w_ref[:, 0:1024])

    lane = lax.broadcasted_iota(jnp.int32, (1, 128), 1)
    rate, bias = jnp.zeros((1, 128), F32), jnp.zeros((1, 128), F32)
    for n in range(4):
        rate = jnp.where(lane == n, rate_ref[n // 2, n % 2], rate)
        bias = jnp.where(lane == n, bias_ref[n // 2, n % 2], bias)
    biased = gates + bias
    soft = jnp.maximum(biased, 0.0) + jnp.log(1.0 + jnp.exp(-jnp.abs(biased)))
    beta = 1.0 / (1.0 + jnp.exp(-gates))
    is_decay, is_beta = lane < 4, (lane >= 4) & (lane < 8)
    ri = lax.broadcasted_iota(jnp.int32, (ROWS, ROWS), 0)
    ci = lax.broadcasted_iota(jnp.int32, (ROWS, ROWS), 1)
    same = (ri // CH) == (ci // CH)
    tri = jnp.where(same & (ri >= ci), 1.0, 0.0).astype(BF16)

    def thirds(v):
        hi = v.astype(BF16).astype(F32)
        rest = v - hi
        mid = rest.astype(BF16).astype(F32)
        return (hi + pltpu.roll(mid, 8, axis=1) + pltpu.roll(rest - mid, 16, axis=1)).astype(BF16)

    sums = mm(tri, thirds(jnp.where(is_decay, -rate * soft, 0.0)))
    sums = sums + pltpu.roll(sums, 120, axis=1) + pltpu.roll(sums, 112, axis=1)
    both = thirds(jnp.where(is_decay, sums, jnp.where(is_beta, beta, 0.0)))

    def spread(first, width):
        r = lax.broadcasted_iota(jnp.int32, (128, 4 * width), 0)
        c = lax.broadcasted_iota(jnp.int32, (128, 4 * width), 1)
        return jnp.where((r < 24) & (r % 8 == c // width + first), 1.0, 0.0).astype(BF16)

    tot_w = mm(both, spread(0, CH))
    beta_w = mm(both, spread(4, CH))
    tot_v = mm(both, spread(0, 128))
    beta_v = mm(both, spread(4, 128))
    grow_v = jnp.exp(tot_v)

    mixed = []
    taps = [taps_ref[i].astype(F32) for i in range(4)]
    for c in range(4):
        acc = None
        for i in range(4):
            term = taps[i][c : c + 1] * pscr[8 - i : 8 - i + ROWS, c * 256 : (c + 1) * 256]
            acc = term if acc is None else acc + term
        mixed.append(silu(acc))

    def unit(v):
        parts = []
        for h in range(2):
            p = v[:, h * 128 : (h + 1) * 128]
            parts.append(p * lax.rsqrt(jnp.sum(p * p, axis=-1, keepdims=True) + 1e-6))
        return jnp.concatenate(parts, axis=1)

    query = (unit(mixed[0]) * (128.0 ** -0.5)).astype(BF16)
    keys_f = unit(mixed[1])
    keys = keys_f.astype(BF16)

    wi = lax.broadcasted_iota(jnp.int32, (CH, 256), 0)
    wj = lax.broadcasted_iota(jnp.int32, (CH, 256), 1) % CH
    eye = wi == wj
    lower = wi >= wj
    strict = wi > wj
    bd_mask = same
    kmask = (lax.broadcasted_iota(jnp.int32, (128, 256), 0) // CH) == (
        lax.broadcasted_iota(jnp.int32, (128, 256), 1) // 128
    )

    def bd(v):
        vb = v.astype(BF16)
        return jnp.where(bd_mask, jnp.concatenate([vb] * 4, axis=0), jnp.zeros((), BF16))

    chunks = range(NG)
    rows = [slice(c * CH, (c + 1) * CH) for c in chunks]
    sys_w, score_w = [], []
    for c in chunks:
        k_c, q_c = keys[rows[c]], query[rows[c]]
        k_bd = jnp.where(kmask, jnp.concatenate([k_c, k_c], axis=0), jnp.zeros((), BF16))
        both = mm_nt(jnp.concatenate([k_c, q_c], axis=0), k_bd)
        kk = jnp.concatenate([both[:CH], both[:CH]], axis=1)
        qk = jnp.concatenate([both[CH:], both[CH:]], axis=1)
        t_c = tot_w[rows[c]]
        t_row = jnp.sum(jnp.where(eye, t_c, 0.0), axis=0, keepdims=True)
        inside = jnp.where(lower, jnp.exp(jnp.where(lower, t_c - t_row, 0.0)), 0.0)
        sys_w.append(jnp.where(strict, beta_w[rows[c]] * kk * inside, 0.0))
        score_w.append(qk * inside)

    eye_f = jnp.where(eye, 1.0, 0.0)

    def block(n):
        return (wi // n) == (wj // n)

    base = [jnp.where(block(8), a, 0.0) for a in sys_w]
    base2 = [mm(d.astype(BF16), bd(d)) for d in base]
    base4 = [mm(d.astype(BF16), bd(d)) for d in base2]
    inv = [eye_f - d for d in base]
    inv = [t + mm(t.astype(BF16), bd(d)) for t, d in zip(inv, base2)]
    inv = [t + mm(t.astype(BF16), bd(d)) for t, d in zip(inv, base4)]
    for n in (16, 32, 64):
        pick = block(n) & jnp.logical_not(block(n // 2))
        low = [jnp.where(pick, a, 0.0).astype(BF16) for a in sys_w]
        mid = [mm(l, bd(t)) for l, t in zip(low, inv)]
        inv = [t - mm(t.astype(BF16), bd(m)) for t, m in zip(inv, mid)]
    fixed = []
    for c in chunks:
        a_hi = sys_w[c].astype(BF16)
        a_lo = (sys_w[c] - a_hi.astype(F32)).astype(BF16)
        t_hi = inv[c].astype(BF16)
        t_lo = (inv[c] - t_hi.astype(F32)).astype(BF16)
        both = mm(jnp.concatenate([a_hi, a_lo], axis=0), bd(t_hi))
        prod = both[:CH] + both[CH:] + mm(a_hi, bd(t_lo))
        resid = eye_f - inv[c] - prod
        fixed.append(inv[c] + mm(t_hi, bd(resid)))
    inv = fixed

    solved = []
    for c in chunks:
        parts = []
        for s in range(2):
            for h in range(2):
                n = s * 2 + h
                b = beta_v[rows[c], n * 128 : (n + 1) * 128]
                g = grow_v[rows[c], n * 128 : (n + 1) * 128]
                v = mixed[2 + s][rows[c], h * 128 : (h + 1) * 128]
                k = keys_f[rows[c], h * 128 : (h + 1) * 128]
                parts.append(jnp.concatenate([(b * v).astype(BF16), (b * g * k).astype(BF16)], axis=1))
        rhs = jnp.concatenate(parts, axis=0)
        solved.append(mm(bd(inv[c]), rhs))
    score_bd = [bd(s) for s in score_w]

    for c in chunks:
        reads = []
        for h in range(2):
            lhs = jnp.concatenate(
                [
                    solved[c][h * CH : (h + 1) * CH, 128:256].astype(BF16),
                    solved[c][(2 + h) * CH : (3 + h) * CH, 128:256].astype(BF16),
                    query[rows[c], h * 128 : (h + 1) * 128],
                ],
                axis=0,
            )
            reads.append(mm(lhs, state[h].astype(BF16)))
        updates, writes = [None] * 4, [None] * 4
        last = tot_v[(c + 1) * CH - 1 : (c + 1) * CH, :]
        for s in range(2):
            for h in range(2):
                n = s * 2 + h
                u = solved[c][n * CH : (n + 1) * CH, 0:128] - reads[h][s * CH : (s + 1) * CH, s * 128 : (s + 1) * 128]
                carry = jnp.exp(last[:, n * 128 : (n + 1) * 128] - tot_v[rows[c], n * 128 : (n + 1) * 128])
                updates[n] = u.astype(BF16)
                writes[n] = (carry * u).astype(BF16)
        for h in range(2):
            decay_all = jnp.concatenate(
                [jnp.exp(last[:, h * 128 : (h + 1) * 128]), jnp.exp(last[:, (2 + h) * 128 : (3 + h) * 128])], axis=1
            )
            write = jnp.concatenate([writes[h], writes[2 + h]], axis=1)
            state[h] = decay_all * state[h] + mm_tn(keys[rows[c], h * 128 : (h + 1) * 128], write)
        inner = mm(score_bd[c], jnp.concatenate(updates, axis=0))
        for s in range(2):
            for h in range(2):
                n = s * 2 + h
                oscr[rows[c], n * 128 : (n + 1) * 128] = (
                    grow_v[rows[c], n * 128 : (n + 1) * 128] * reads[h][2 * CH :, s * 128 : (s + 1) * 128]
                    + inner[n * CH : (n + 1) * CH]
                )

    og = mm(x, w_ref[:, 1024:1536])
    hidden = []
    for n in range(4):
        r = oscr[:, n * 128 : (n + 1) * 128]
        r = r * lax.rsqrt(jnp.mean(r * r, axis=-1, keepdims=True) + 1e-6) * gain_ref[...]
        hidden.append((r * silu(og[:, n * 128 : (n + 1) * 128])).astype(BF16))
    hidden = jnp.concatenate(hidden, axis=1)
    p_ref[pl.ds(pl.multiple_of(step * ROWS, ROWS), ROWS), :] = mm_nt(hidden, w_ref[:, 1664:2176]).astype(BF16)

    @pl.when(step == 2)
    def _():
        across.relay(0)

    @pl.when(step == 3)
    def _():
        across.begin(1)
        across.total(0)
        across.relay(1)
        across.pass_on(0)
        across.total(1)
        across.pass_on(1)
        across.finish(out_ref)


def mixer(x, w, taps, rate, bias, gain):
    seq, width = x.shape
    whole = lambda i: (0, 0)
    return pl.pallas_call(
        mixer_kernel,
        grid=(seq // ROWS,),
        out_shape=jax.ShapeDtypeStruct((seq // 8, width), BF16),
        in_specs=[
            pl.BlockSpec((ROWS, 2048), lambda i: (i, 0)),
            pl.BlockSpec((2048, 2176), whole, pipeline_mode=pl.Buffered(1)),
            pl.BlockSpec((4, 4, 256), lambda i: (0, 0, 0)),
            pl.BlockSpec(memory_space=pltpu.SMEM),
            pl.BlockSpec(memory_space=pltpu.SMEM),
            pl.BlockSpec((1, 128), whole),
        ],
        out_specs=pl.BlockSpec((seq // 8, width), whole),
        scratch_shapes=[
            pltpu.VMEM((ROWS + 8, 1024), F32),
            pltpu.VMEM((ROWS, 512), F32),
            pltpu.VMEM((2, 128, 256), F32),
            pltpu.VMEM((seq, width), BF16),
            pltpu.VMEM((2, 2, 64, width), BF16),
            pltpu.VMEM((2, 2, 2, 64, width), BF16),
            pltpu.VMEM((2, 2, 64, width), BF16),
            pltpu.VMEM((2, 64, width), F32),
            pltpu.VMEM((2, 64, width), BF16),
            pltpu.VMEM((2, 64, width), BF16),
            pltpu.VMEM((2, 64, width), BF16),
            DMA((17,)), DMA((17,)),
        ],
        compiler_params=pltpu.CompilerParams(collective_id=1, has_side_effects=True, vmem_limit_bytes=52 << 20),
        name="mixer",
    )(x, w, taps, rate, bias, gain)


def body(
    prompt_states,
    lengths,
    bucket_owner,
    w_in,
    w_gates,
    out_weight,
    conv_weight,
    decay_rate,
    dt_bias,
    in_gain,
    head_gain,
):
    tok_rows = prompt_states.shape[1]
    rows = w_in.shape[0]
    normed = prep(bucket_owner, prompt_states[0], in_gain[None, :])
    packed = jnp.concatenate(
        [
            w_in.reshape(rows, -1),
            jnp.pad(w_gates.reshape(rows, -1), ((0, 0), (0, 120))),
            out_weight.reshape(rows, -1),
        ],
        axis=1,
    )
    full_rows, weights = gather(normed, packed)
    mine = mixer(full_rows, weights, conv_weight, decay_rate, dt_bias, head_gain[None, :])
    live = lengths - lax.axis_index("tp") * tok_rows
    return finish(bucket_owner, live, mine)[None]


def solution(mesh):
    in_specs = (
        P("roll", "tp", None),
        P("roll"),
        P(),
        P("roll", None, "tp"),
        P("roll", None, None, "tp"),
        P("roll", None, "tp"),
        P(None, None, "tp"),
        P(None, "tp"),
        P(None, "tp"),
        P(),
        P(),
    )
    out_specs = P("roll", "tp", None)
    return jax.shard_map(body, mesh=mesh, in_specs=in_specs, out_specs=out_specs, check_vma=False)
```

```python
import jax
import jax.numpy as jnp
from jax import lax
from jax.experimental import pallas as pl
from jax.experimental.pallas import tpu as pltpu
from jax.sharding import PartitionSpec as P

CH = 64
NG = 4
ROWS = CH * NG
F32 = jnp.float32
BF16 = jnp.bfloat16
HIGHEST = lax.Precision.HIGHEST


def mm(a, b):
    return jnp.dot(a, b, preferred_element_type=F32)


def mm_nt(a, b):
    return lax.dot_general(a, b, (((1,), (1,)), ((), ())), preferred_element_type=F32)


def mm_tn(a, b):
    return lax.dot_general(a, b, (((0,), (0,)), ((), ())), preferred_element_type=F32)


def mm_exact(a, b):
    return jnp.dot(a, b, preferred_element_type=F32, precision=HIGHEST)


def silu(v):
    return v / (1.0 + jnp.exp(-v))


def prep_kernel(owner_ref, x_ref, gain_ref, out_ref, scr, inverse):
    x = x_ref[...].astype(F32)
    scale = lax.rsqrt(jnp.mean(x * x, axis=-1, keepdims=True) + 1e-6)
    scr[...] = x * scale * gain_ref[...]
    for b in range(32):
        inverse[owner_ref[b]] = b
    low = lax.broadcasted_iota(jnp.int32, (128, 128), 1) < 64

    def half(block, side):
        tile = scr[:, pl.ds(pl.multiple_of((block // 2) * 128, 128), 128)]
        return jnp.where(block % 2 == side, tile, pltpu.roll(tile, 64, axis=1))

    for j in range(16):
        out_ref[:, j * 128 : (j + 1) * 128] = jnp.where(
            low, half(inverse[2 * j], 0), half(inverse[2 * j + 1], 1)
        ).astype(BF16)


def prep(owner, x, gain):
    return pl.pallas_call(
        prep_kernel,
        out_shape=jax.ShapeDtypeStruct(x.shape, BF16),
        in_specs=[
            pl.BlockSpec(memory_space=pltpu.SMEM),
            pl.BlockSpec(memory_space=pltpu.VMEM),
            pl.BlockSpec(memory_space=pltpu.VMEM),
        ],
        out_specs=pl.BlockSpec(memory_space=pltpu.VMEM),
        scratch_shapes=[pltpu.VMEM(x.shape, F32), pltpu.SMEM((32,), jnp.int32)],
        name="prep",
    )(owner, x, gain)


def finish_kernel(owner_ref, live_ref, x_ref, out_ref, scr):
    scr[...] = x_ref[...].astype(F32)
    live = lax.broadcasted_iota(jnp.int32, (128, 128), 0) < live_ref[0]
    low = lax.broadcasted_iota(jnp.int32, (128, 128), 1) < 64

    def half(block, side):
        tile = scr[:, pl.ds(pl.multiple_of((block // 2) * 128, 128), 128)]
        return jnp.where(block % 2 == side, tile, pltpu.roll(tile, 64, axis=1))

    for j in range(16):
        tile = jnp.where(low, half(owner_ref[2 * j], 0), half(owner_ref[2 * j + 1], 1))
        out_ref[:, j * 128 : (j + 1) * 128] = jnp.where(live, tile, 0.0).astype(BF16)


def finish(owner, live, x):
    return pl.pallas_call(
        finish_kernel,
        out_shape=jax.ShapeDtypeStruct(x.shape, BF16),
        in_specs=[
            pl.BlockSpec(memory_space=pltpu.SMEM),
            pl.BlockSpec(memory_space=pltpu.SMEM),
            pl.BlockSpec(memory_space=pltpu.VMEM),
        ],
        out_specs=pl.BlockSpec(memory_space=pltpu.VMEM),
        scratch_shapes=[pltpu.VMEM(x.shape, F32)],
        name="finish",
    )(owner, live, x)


MESH = pl.DeviceIdType.MESH


class Place:
    def __init__(self):
        roll, tp = lax.axis_index("roll"), lax.axis_index("tp")
        self.zl, self.x, self.core = roll // 8, (roll // 2) % 4, roll % 2
        self.zh, self.y = tp // 4, tp % 4

    def at(self, zl=None, x=None, core=None, zh=None, y=None):
        zl = self.zl if zl is None else zl
        x = self.x if x is None else x
        core = self.core if core is None else core
        zh = self.zh if zh is None else zh
        y = self.y if y is None else y
        return (zl * 8 + x * 2 + core, zh * 4 + y)

    def along_z(self, hops):
        z = (self.zh * 4 + self.zl + hops) % 8
        return self.at(zl=z % 4, zh=z // 4)


def meet(devices):
    barrier = pltpu.get_barrier_semaphore()
    for device in devices:
        pl.semaphore_signal(barrier, inc=1, device_id=device, device_id_type=MESH)
    pl.semaphore_wait(barrier, len(devices))


class Pull:
    def __init__(self, x_ref, w_refs, xo, wos, transit, zs_up, zs_dn, zr, ws, wr, ys, yr, own_sem):
        self.x_ref, self.w_refs, self.xo, self.wos, self.transit = x_ref, w_refs, xo, wos, transit
        self.zs_up, self.zs_dn, self.zr, self.ws, self.wr = zs_up, zs_dn, zr, ws, wr
        self.ys, self.yr, self.own_sem = ys, yr, own_sem
        me = self.me = Place()
        self.xl, self.xr, self.xf = (me.x + 3) % 4, (me.x + 1) % 4, (me.x + 2) % 4
        self.yl, self.yn, self.yf = (me.y + 3) % 4, (me.y + 1) % 4, (me.y + 2) % 4
        self.left_x, self.right_x = me.at(x=self.xl), me.at(x=self.xr)
        self.left_y, self.right_y = me.at(y=self.yl), me.at(y=self.yn)
        self.up, self.down = me.at(zl=(me.zl + 1) % 4), me.at(zl=(me.zl + 3) % 4)
        self.sibling, self.partner = me.at(core=1 - me.core), me.at(zh=1 - me.zh)
        self.behind, self.ahead = me.along_z(6), me.along_z(2)
        self.away_to = me.along_z(jnp.where(me.zh == 0, 6, 2))
        self.outer = (me.zh * 4 + me.zl + 2) % 8 < 4
        self.other = 1 - me.zh
        order = [[0, 1, 2, 3], [1, 2, 0, 3], [2, 1, 3, 0], [3, 2, 1, 0]]
        self.slot = [
            jnp.where(
                me.zl == 0,
                order[0][j],
                jnp.where(me.zl == 1, order[1][j], jnp.where(me.zl == 2, order[2][j], order[3][j])),
            )
            for j in range(4)
        ]

    def meet(self):
        meet(
            [self.left_x, self.right_x, self.left_y, self.right_y, self.up, self.down]
            + [self.sibling, self.partner, self.behind, self.ahead]
        )

    def copy(self, src, dst, send, recv, device):
        return pltpu.make_async_remote_copy(
            src_ref=src, dst_ref=dst, send_sem=send, recv_sem=recv, device_id=device, device_id_type=MESH
        )

    def shard(self, w, z, x, core):
        return self.wos[w].at[pl.ds(pl.multiple_of((z * 8 + x * 2 + core) * 64, 64), 64)]

    def part(self, w, z, x, core, p):
        return self.wos[w].at[pl.ds(pl.multiple_of((z * 8 + x * 2 + core) * 64 + p * 32, 32), 32)]

    def z_copy(self, w, z, src, upward):
        i = w * 4 + z
        dst = self.shard(w, z, self.me.x, self.me.core)
        sems, device = (self.zs_up, self.up) if upward else (self.zs_dn, self.down)
        return self.copy(src, dst, sems.at[i], self.zr.at[i], device)

    def start_z(self, w):
        for upward, has in ((True, self.me.zl < 3), (False, self.me.zl > 0)):

            @pl.when(has)
            def _():
                self.z_copy(w, self.me.zl, self.w_refs[w], upward).start()

    def take_z(self, w, j):
        me, z = self.me, self.slot[j]
        here = self.shard(w, z, me.x, me.core)
        self.z_copy(w, z, here, True).wait_recv()
        for upward, on in ((True, (z < me.zl) & (me.zl < 3)), (False, (z > me.zl) & (me.zl > 0))):

            @pl.when(on)
            def _():
                self.z_copy(w, z, self.shard(w, z, me.x, me.core), upward).start()

    def w_msg(self, w, j, i):
        me, z = self.me, self.slot[j]
        own = self.shard(w, z, me.x, me.core)
        src, dst, device = (
            (self.w_refs[w] if j == 0 else own, own, self.right_x),
            (self.w_refs[w] if j == 0 else own, own, self.left_x),
            (self.part(w, z, self.xl, me.core, 0),) * 2 + (self.right_x,),
            (self.part(w, z, self.xr, me.core, 1),) * 2 + (self.left_x,),
            (self.w_refs[w] if j == 0 else own, own, self.sibling),
            (self.shard(w, z, self.xl, me.core),) * 2 + (self.sibling,),
            (self.shard(w, z, self.xr, me.core),) * 2 + (self.sibling,),
            (self.shard(w, z, self.xf, me.core),) * 2 + (self.sibling,),
        )[i]
        n = w * 32 + j * 8 + i
        return self.copy(src, dst, self.ws.at[n], self.wr.at[n], device)

    def w_wait(self, w, j, i):
        me, z = self.me, self.slot[j]
        dst = (
            lambda: self.shard(w, z, self.xl, me.core),
            lambda: self.shard(w, z, self.xr, me.core),
            lambda: self.part(w, z, self.xf, me.core, 0),
            lambda: self.part(w, z, self.xf, me.core, 1),
            lambda: self.shard(w, z, me.x, 1 - me.core),
            lambda: self.shard(w, z, self.xl, 1 - me.core),
            lambda: self.shard(w, z, self.xr, 1 - me.core),
            lambda: self.shard(w, z, self.xf, 1 - me.core),
        )[i]()
        n = w * 32 + j * 8 + i
        self.copy(dst, dst, self.ws.at[n], self.wr.at[n], self.sibling).wait_recv()

    def spread_x(self, w, j):
        for i in (0, 1, 4):
            self.w_msg(w, j, i).start()

    def relay_x(self, w, j):
        self.w_wait(w, j, 0)
        self.w_msg(w, j, 2).start()
        self.w_wait(w, j, 1)
        self.w_msg(w, j, 3).start()
        self.w_msg(w, j, 5).start()
        self.w_msg(w, j, 6).start()

    def far_x(self, w, j):
        self.w_wait(w, j, 2)
        self.w_wait(w, j, 3)
        self.w_msg(w, j, 7).start()

    def siblings(self, w):
        for j in range(4):
            for i in range(4, 8):
                self.w_wait(w, j, i)

    def block(self, zh, y, p):
        return self.xo.at[pl.ds(pl.multiple_of((zh * 4 + y) * 128 + p * 64, 64), 64)]

    def y_msg(self, b, k):
        me = self.me
        zh = self.other if b else me.zh
        if k < 4:
            dst = self.block(zh, me.y, k % 2)
            src = dst if b else self.x_ref.at[pl.ds(k % 2 * 64, 64)]
            device = self.right_y if k < 2 else self.left_y
        else:
            dst = src = self.block(zh, self.yl if k == 4 else self.yn, k - 4)
            device = self.right_y if k == 4 else self.left_y
        return self.copy(src, dst, self.ys.at[b * 6 + k], self.yr.at[b * 6 + k], device)

    def y_wait(self, b, k):
        zh = self.other if b else self.me.zh
        y, p = ((self.yl, 0), (self.yl, 1), (self.yn, 0), (self.yn, 1), (self.yf, 0), (self.yf, 1))[k]
        dst = self.block(zh, y, p)
        self.copy(dst, dst, self.ys.at[b * 6 + k], self.yr.at[b * 6 + k], self.partner).wait_recv()

    def relay_y(self, b):
        self.y_wait(b, 0)
        self.y_msg(b, 4).start()
        self.y_wait(b, 3)
        self.y_msg(b, 5).start()

    def rest_y(self, b):
        for k in (1, 2, 4, 5):
            self.y_wait(b, k)

    def direct(self):
        return self.copy(
            self.x_ref.at[pl.ds(0, 64)], self.block(self.me.zh, self.me.y, 0), self.ys.at[12], self.yr.at[12], self.partner
        )

    def away(self):
        i = 13 + 2 * self.me.zh
        return self.copy(
            self.x_ref.at[pl.ds(64, 64)], self.transit.at[self.me.zh], self.ys.at[i], self.yr.at[i], self.away_to
        )

    def onward(self, s):
        i = 14 + 2 * s
        return self.copy(
            self.transit.at[s], self.block(s, self.me.y, 1), self.ys.at[i], self.yr.at[i], self.ahead if s else self.behind
        )

    def pass_on(self):
        @pl.when(self.outer)
        def _():
            for s in range(2):
                i = 13 + 2 * s
                dst = self.transit.at[s]
                self.copy(dst, dst, self.ys.at[i], self.yr.at[i], self.partner).wait_recv()
                self.onward(s).start()

    def take_other(self, p):
        i = 14 + 2 * self.other if p else 12
        dst = self.block(self.other, self.me.y, p)
        self.copy(dst, dst, self.ys.at[i], self.yr.at[i], self.partner).wait_recv()
        self.y_msg(1, p).start()
        self.y_msg(1, 2 + p).start()

    def open(self):
        me = self.me
        self.meet()
        self.start_z(0)
        self.spread_x(0, 0)
        self.away().start()
        self.direct().start()
        for k in (0, 2, 1, 3):
            self.y_msg(0, k).start()
        keep = [
            pltpu.make_async_copy(self.w_refs[w], self.shard(w, me.zl, me.x, me.core), self.own_sem.at[w])
            for w in range(2)
        ]
        rows = pl.ds(pl.multiple_of((me.zh * 4 + me.y) * 128, 128), 128)
        keep.append(pltpu.make_async_copy(self.x_ref, self.xo.at[rows], self.own_sem.at[2]))
        for c in keep:
            c.start()
        for j in (1, 2, 3):
            self.take_z(0, j)
            self.spread_x(0, j)
            self.relay_x(0, j - 1)
            if j == 2:
                self.relay_y(0)
                self.pass_on()
        self.start_z(1)
        self.far_x(0, 0)
        self.take_other(0)
        self.far_x(0, 1)
        self.take_other(1)
        self.relay_x(0, 3)
        self.take_z(1, 1)
        self.far_x(0, 2)
        self.take_z(1, 2)

        @pl.when(me.zh == 1)
        def _():
            self.relay_y(1)

        self.far_x(0, 3)
        self.take_z(1, 3)
        for j in range(4):
            self.spread_x(1, j)

        @pl.when(me.zh == 0)
        def _():
            self.rest_y(0)

        @pl.when(me.zh == 1)
        def _():
            self.rest_y(1)

        self.siblings(0)
        for c in keep:
            c.wait()

    def second(self):
        @pl.when(self.me.zh == 0)
        def _():
            self.relay_y(1)

        for j in range(4):
            self.relay_x(1, j)

    def third(self):
        for j in range(4):
            self.far_x(1, j)

    def later_half(self):
        @pl.when(self.me.zh == 0)
        def _():
            self.rest_y(1)

        @pl.when(self.me.zh == 1)
        def _():
            self.rest_y(0)

    def close(self):
        me = self.me
        for w in range(2):
            for j in range(4):
                z = self.slot[j]
                for i in range(8):
                    self.w_msg(w, j, i).wait_send()
                for upward, on in ((True, (z <= me.zl) & (me.zl < 3)), (False, (z >= me.zl) & (me.zl > 0))):

                    @pl.when(on)
                    def _():
                        self.z_copy(w, z, self.shard(w, z, me.x, me.core), upward).wait_send()

        for b in range(2):
            for k in range(6):
                self.y_msg(b, k).wait_send()
        self.direct().wait_send()
        self.away().wait_send()

        @pl.when(self.outer)
        def _():
            for s in range(2):
                self.onward(s).wait_send()


DMA = pltpu.SemaphoreType.DMA


class Sums:
    def __init__(self, p_ref, first, full, mixed, kept, summed, landed, transit, ss, rs):
        self.p, self.first, self.full, self.mixed = p_ref, first, full, mixed
        self.kept, self.summed, self.landed, self.transit = kept, summed, landed, transit
        self.ss, self.rs = ss, rs
        me = self.me = Place()
        self.left, self.right = me.at(y=(me.y + 3) % 4), me.at(y=(me.y + 1) % 4)
        self.partner, self.behind, self.ahead = me.at(zh=1 - me.zh), me.along_z(6), me.along_z(2)
        self.outer = (me.zh * 4 + me.zl + 2) % 8 < 4

    def copy(self, i, src, dst, device):
        return pltpu.make_async_remote_copy(
            src_ref=src, dst_ref=dst, send_sem=self.ss.at[i], recv_sem=self.rs.at[i], device_id=device, device_id_type=MESH
        )

    def half(self, b, y, p):
        return self.p.at[pl.ds(pl.multiple_of((b * 4 + y) * 128 + p * 64, 64), 64)]

    def message(self, b, k):
        y, first, full = self.me.y, self.first, self.full
        far, right, left = (y + 2) % 4, (y + 1) % 4, (y + 3) % 4
        src, dst = (
            (self.half(b, far, 0), first.at[b, 0]),
            (self.half(b, far, 1), first.at[b, 1]),
            (self.half(b, right, 1), full.at[b, 0, 1]),
            (self.half(b, left, 0), full.at[b, 1, 0]),
            (self.mixed.at[b, 0], full.at[b, 0, 0]),
            (self.mixed.at[b, 1], full.at[b, 1, 1]),
        )[k]
        return self.copy(b * 6 + k, src, dst, self.left if k % 2 else self.right)

    def begin(self, b):
        for k in range(4):
            self.message(b, k).start()

    def relay(self, b):
        y = self.me.y
        for p, near in ((0, (y + 1) % 4), (1, (y + 3) % 4)):
            self.message(b, p).wait_recv()
            self.mixed[b, p] = (self.half(b, near, p)[...].astype(F32) + self.first[b, p].astype(F32)).astype(BF16)
            self.message(b, 4 + p).start()

    def across(self, b, p):
        if p == 0:
            return self.copy(12, self.summed.at[0], self.landed.at[0], self.partner)
        return self.copy(13 + 2 * b, self.summed.at[1], self.transit.at[b], self.behind if b else self.ahead)

    def passing(self, b):
        return self.copy(14 + 2 * b, self.transit.at[b], self.landed.at[1], self.behind if b else self.ahead)

    def total(self, b):
        for p in (1, 0):
            for k in ((3, 4), (2, 5))[p]:
                self.message(b, k).wait_recv()
            value = (
                self.half(b, self.me.y, p)[...].astype(F32)
                + self.full[b, 0, p].astype(F32)
                + self.full[b, 1, p].astype(F32)
            )

            @pl.when(self.me.zh == b)
            def _():
                self.kept[p] = value

            @pl.when(self.me.zh != b)
            def _():
                self.summed[p] = value.astype(BF16)
                self.across(b, p).start()

    def pass_on(self, b):
        @pl.when(self.outer)
        def _():
            self.across(b, 1).wait_recv()
            self.passing(b).start()

    def finish(self, out_ref):
        self.across(0, 0).wait_recv()
        for b in range(2):

            @pl.when(self.me.zh == b)
            def _():
                self.passing(b).wait_recv()

        for p in range(2):
            out_ref[p * 64 : (p + 1) * 64, :] = (self.kept[p] + self.landed[p].astype(F32)).astype(BF16)
        for b in range(2):
            for k in range(6):
                self.message(b, k).wait_send()
        self.across(0, 0).wait_send()
        for b in range(2):

            @pl.when(self.me.zh != b)
            def _():
                self.across(b, 1).wait_send()

            @pl.when(self.outer)
            def _():
                self.passing(b).wait_send()


def mixer_kernel(
    own_ref, w1_ref, w2_ref, taps_ref, rate_ref, bias_ref, gain_ref, out_ref,
    x_ref, w_ref, wout_ref, hid, passing, zs_up, zs_dn, zr, ws, wr, ys, yr, own_sem,
    pscr, oscr, state, p_ref, first, full, mixed, kept, summed, landed, transit, ss, rs,
):
    step = pl.program_id(0)
    across = Sums(p_ref, first, full, mixed, kept, summed, landed, transit, ss, rs)

    pull = Pull(
        own_ref, (w1_ref, w2_ref), x_ref, (w_ref, wout_ref), passing, zs_up, zs_dn, zr, ws, wr, ys, yr, own_sem
    )

    @pl.when(step == 0)
    def _():
        pull.open()

    @pl.when(step == 1)
    def _():
        pull.second()

    @pl.when(step == 2)
    def _():
        across.begin(0)
        pull.later_half()


    @pl.when(step == 0)
    def _():
        pscr[0:8, :] = jnp.zeros((8, 1024), F32)
        state[...] = jnp.zeros_like(state)

    @pl.when(step > 0)
    def _():
        pscr[0:8, :] = pscr[ROWS : ROWS + 8, :]

    here = pl.ds(pl.multiple_of(step * ROWS, ROWS), ROWS)
    x = x_ref[here, :]
    gates = mm(x, w_ref[:, 1536:1664])
    pscr[8 : 8 + ROWS, :] = mm(x, w_ref[:, 0:1024])

    @pl.when(step == 1)
    def _():
        pull.third()


    lane = lax.broadcasted_iota(jnp.int32, (1, 128), 1)
    rate, bias = jnp.zeros((1, 128), F32), jnp.zeros((1, 128), F32)
    for n in range(4):
        rate = jnp.where(lane == n, rate_ref[n // 2, n % 2], rate)
        bias = jnp.where(lane == n, bias_ref[n // 2, n % 2], bias)
    biased = gates + bias
    soft = jnp.maximum(biased, 0.0) + jnp.log(1.0 + jnp.exp(-jnp.abs(biased)))
    beta = 1.0 / (1.0 + jnp.exp(-gates))
    is_decay, is_beta = lane < 4, (lane >= 4) & (lane < 8)
    ri = lax.broadcasted_iota(jnp.int32, (ROWS, ROWS), 0)
    ci = lax.broadcasted_iota(jnp.int32, (ROWS, ROWS), 1)
    same = (ri // CH) == (ci // CH)
    tri = jnp.where(same & (ri >= ci), 1.0, 0.0).astype(BF16)

    def thirds(v):
        hi = v.astype(BF16).astype(F32)
        rest = v - hi
        mid = rest.astype(BF16).astype(F32)
        return (hi + pltpu.roll(mid, 8, axis=1) + pltpu.roll(rest - mid, 16, axis=1)).astype(BF16)

    sums = mm(tri, thirds(jnp.where(is_decay, -rate * soft, 0.0)))
    sums = sums + pltpu.roll(sums, 120, axis=1) + pltpu.roll(sums, 112, axis=1)
    both = thirds(jnp.where(is_decay, sums, jnp.where(is_beta, beta, 0.0)))

    def spread(first, width):
        r = lax.broadcasted_iota(jnp.int32, (128, 4 * width), 0)
        c = lax.broadcasted_iota(jnp.int32, (128, 4 * width), 1)
        return jnp.where((r < 24) & (r % 8 == c // width + first), 1.0, 0.0).astype(BF16)

    tot_w = mm(both, spread(0, CH))
    beta_w = mm(both, spread(4, CH))
    tot_v = mm(both, spread(0, 128))
    beta_v = mm(both, spread(4, 128))
    grow_v = jnp.exp(tot_v)

    mixed = []
    taps = [taps_ref[i].astype(F32) for i in range(4)]
    for c in range(4):
        acc = None
        for i in range(4):
            term = taps[i][c : c + 1] * pscr[8 - i : 8 - i + ROWS, c * 256 : (c + 1) * 256]
            acc = term if acc is None else acc + term
        mixed.append(silu(acc))

    def unit(v):
        parts = []
        for h in range(2):
            p = v[:, h * 128 : (h + 1) * 128]
            parts.append(p * lax.rsqrt(jnp.sum(p * p, axis=-1, keepdims=True) + 1e-6))
        return jnp.concatenate(parts, axis=1)

    query = (unit(mixed[0]) * (128.0 ** -0.5)).astype(BF16)
    keys_f = unit(mixed[1])
    keys = keys_f.astype(BF16)

    wi = lax.broadcasted_iota(jnp.int32, (CH, 256), 0)
    wj = lax.broadcasted_iota(jnp.int32, (CH, 256), 1) % CH
    eye = wi == wj
    lower = wi >= wj
    strict = wi > wj
    bd_mask = same
    kmask = (lax.broadcasted_iota(jnp.int32, (128, 256), 0) // CH) == (
        lax.broadcasted_iota(jnp.int32, (128, 256), 1) // 128
    )

    def bd(v):
        vb = v.astype(BF16)
        return jnp.where(bd_mask, jnp.concatenate([vb] * 4, axis=0), jnp.zeros((), BF16))

    chunks = range(NG)
    rows = [slice(c * CH, (c + 1) * CH) for c in chunks]
    sys_w, score_w = [], []
    for c in chunks:
        k_c, q_c = keys[rows[c]], query[rows[c]]
        k_bd = jnp.where(kmask, jnp.concatenate([k_c, k_c], axis=0), jnp.zeros((), BF16))
        both = mm_nt(jnp.concatenate([k_c, q_c], axis=0), k_bd)
        kk = jnp.concatenate([both[:CH], both[:CH]], axis=1)
        qk = jnp.concatenate([both[CH:], both[CH:]], axis=1)
        t_c = tot_w[rows[c]]
        t_row = jnp.sum(jnp.where(eye, t_c, 0.0), axis=0, keepdims=True)
        inside = jnp.where(lower, jnp.exp(jnp.where(lower, t_c - t_row, 0.0)), 0.0)
        sys_w.append(jnp.where(strict, beta_w[rows[c]] * kk * inside, 0.0))
        score_w.append(qk * inside)

    eye_f = jnp.where(eye, 1.0, 0.0)

    def block(n):
        return (wi // n) == (wj // n)

    base = [jnp.where(block(8), a, 0.0) for a in sys_w]
    base2 = [mm(d.astype(BF16), bd(d)) for d in base]
    base4 = [mm(d.astype(BF16), bd(d)) for d in base2]
    inv = [eye_f - d for d in base]
    inv = [t + mm(t.astype(BF16), bd(d)) for t, d in zip(inv, base2)]
    inv = [t + mm(t.astype(BF16), bd(d)) for t, d in zip(inv, base4)]
    for n in (16, 32, 64):
        pick = block(n) & jnp.logical_not(block(n // 2))
        low = [jnp.where(pick, a, 0.0).astype(BF16) for a in sys_w]
        mid = [mm(l, bd(t)) for l, t in zip(low, inv)]
        inv = [t - mm(t.astype(BF16), bd(m)) for t, m in zip(inv, mid)]
    fixed = []
    for c in chunks:
        a_hi = sys_w[c].astype(BF16)
        a_lo = (sys_w[c] - a_hi.astype(F32)).astype(BF16)
        t_hi = inv[c].astype(BF16)
        t_lo = (inv[c] - t_hi.astype(F32)).astype(BF16)
        both = mm(jnp.concatenate([a_hi, a_lo], axis=0), bd(t_hi))
        prod = both[:CH] + both[CH:] + mm(a_hi, bd(t_lo))
        resid = eye_f - inv[c] - prod
        fixed.append(inv[c] + mm(t_hi, bd(resid)))
    inv = fixed

    solved = []
    for c in chunks:
        parts = []
        for s in range(2):
            for h in range(2):
                n = s * 2 + h
                b = beta_v[rows[c], n * 128 : (n + 1) * 128]
                g = grow_v[rows[c], n * 128 : (n + 1) * 128]
                v = mixed[2 + s][rows[c], h * 128 : (h + 1) * 128]
                k = keys_f[rows[c], h * 128 : (h + 1) * 128]
                parts.append(jnp.concatenate([(b * v).astype(BF16), (b * g * k).astype(BF16)], axis=1))
        rhs = jnp.concatenate(parts, axis=0)
        solved.append(mm(bd(inv[c]), rhs))
    score_bd = [bd(s) for s in score_w]

    for c in chunks:
        reads = []
        for h in range(2):
            lhs = jnp.concatenate(
                [
                    solved[c][h * CH : (h + 1) * CH, 128:256].astype(BF16),
                    solved[c][(2 + h) * CH : (3 + h) * CH, 128:256].astype(BF16),
                    query[rows[c], h * 128 : (h + 1) * 128],
                ],
                axis=0,
            )
            reads.append(mm(lhs, state[h].astype(BF16)))
        updates, writes = [None] * 4, [None] * 4
        last = tot_v[(c + 1) * CH - 1 : (c + 1) * CH, :]
        for s in range(2):
            for h in range(2):
                n = s * 2 + h
                u = solved[c][n * CH : (n + 1) * CH, 0:128] - reads[h][s * CH : (s + 1) * CH, s * 128 : (s + 1) * 128]
                carry = jnp.exp(last[:, n * 128 : (n + 1) * 128] - tot_v[rows[c], n * 128 : (n + 1) * 128])
                updates[n] = u.astype(BF16)
                writes[n] = (carry * u).astype(BF16)
        for h in range(2):
            decay_all = jnp.concatenate(
                [jnp.exp(last[:, h * 128 : (h + 1) * 128]), jnp.exp(last[:, (2 + h) * 128 : (3 + h) * 128])], axis=1
            )
            write = jnp.concatenate([writes[h], writes[2 + h]], axis=1)
            state[h] = decay_all * state[h] + mm_tn(keys[rows[c], h * 128 : (h + 1) * 128], write)
        inner = mm(score_bd[c], jnp.concatenate(updates, axis=0))
        for s in range(2):
            for h in range(2):
                n = s * 2 + h
                oscr[rows[c], n * 128 : (n + 1) * 128] = (
                    grow_v[rows[c], n * 128 : (n + 1) * 128] * reads[h][2 * CH :, s * 128 : (s + 1) * 128]
                    + inner[n * CH : (n + 1) * CH]
                )

    og = mm(x, w_ref[:, 1024:1536])
    hidden = []
    for n in range(4):
        r = oscr[:, n * 128 : (n + 1) * 128]
        r = r * lax.rsqrt(jnp.mean(r * r, axis=-1, keepdims=True) + 1e-6) * gain_ref[...]
        hidden.append((r * silu(og[:, n * 128 : (n + 1) * 128])).astype(BF16))
    hidden = jnp.concatenate(hidden, axis=1)
    hid[here, :] = hidden

    @pl.when(step == 1)
    def _():
        pull.siblings(1)
        p_ref[0:ROWS, :] = mm_nt(hid[0:ROWS, :], wout_ref[...]).astype(BF16)

    @pl.when(step > 0)
    def _():
        p_ref[here, :] = mm_nt(hid[here, :], wout_ref[...]).astype(BF16)

    @pl.when(step == 2)
    def _():
        across.relay(0)

    @pl.when(step == 3)
    def _():
        across.begin(1)
        across.total(0)
        across.relay(1)
        across.pass_on(0)
        across.total(1)
        across.pass_on(1)
        across.finish(out_ref)
        pull.close()


def mixer(rows, w1, w2, taps, rate, bias, gain):
    own, width = rows.shape
    seq, depth = own * 8, w1.shape[0] * 32
    whole = lambda i: (0, 0)
    return pl.pallas_call(
        mixer_kernel,
        grid=(seq // ROWS,),
        out_shape=jax.ShapeDtypeStruct(rows.shape, BF16),
        in_specs=[
            pl.BlockSpec(memory_space=pl.ANY),
            pl.BlockSpec(memory_space=pl.ANY),
            pl.BlockSpec(memory_space=pl.ANY),
            pl.BlockSpec((4, 4, 256), lambda i: (0, 0, 0)),
            pl.BlockSpec(memory_space=pltpu.SMEM),
            pl.BlockSpec(memory_space=pltpu.SMEM),
            pl.BlockSpec((1, 128), whole),
        ],
        out_specs=pl.BlockSpec(rows.shape, whole),
        scratch_shapes=[
            pltpu.VMEM((seq, width), BF16),
            pltpu.VMEM((depth, w1.shape[1]), BF16),
            pltpu.VMEM((depth, w2.shape[1]), BF16),
            pltpu.VMEM((seq, 512), BF16),
            pltpu.VMEM((2, 64, width), BF16),
            DMA((8,)), DMA((8,)), DMA((8,)),
            DMA((64,)), DMA((64,)),
            DMA((17,)), DMA((17,)),
            DMA((3,)),
            pltpu.VMEM((ROWS + 8, 1024), F32),
            pltpu.VMEM((ROWS, 512), F32),
            pltpu.VMEM((2, 128, 256), F32),
            pltpu.VMEM((seq, width), BF16),
            pltpu.VMEM((2, 2, 64, width), BF16),
            pltpu.VMEM((2, 2, 2, 64, width), BF16),
            pltpu.VMEM((2, 2, 64, width), BF16),
            pltpu.VMEM((2, 64, width), F32),
            pltpu.VMEM((2, 64, width), BF16),
            pltpu.VMEM((2, 64, width), BF16),
            pltpu.VMEM((2, 64, width), BF16),
            DMA((17,)), DMA((17,)),
        ],
        compiler_params=pltpu.CompilerParams(collective_id=0, has_side_effects=True, vmem_limit_bytes=58 << 20),
        name="mixer",
    )(rows, w1, w2, taps, rate, bias, gain)


def body(
    prompt_states,
    lengths,
    bucket_owner,
    w_in,
    w_gates,
    out_weight,
    conv_weight,
    decay_rate,
    dt_bias,
    in_gain,
    head_gain,
):
    tok_rows = prompt_states.shape[1]
    rows = w_in.shape[0]
    normed = prep(bucket_owner, prompt_states[0], in_gain[None, :])
    packed = jnp.concatenate(
        [w_in.reshape(rows, -1), jnp.pad(w_gates.reshape(rows, -1), ((0, 0), (0, 120)))], axis=1
    )
    mine = mixer(
        normed, packed, out_weight.reshape(rows, -1), conv_weight, decay_rate, dt_bias, head_gain[None, :]
    )
    live = lengths - lax.axis_index("tp") * tok_rows
    return finish(bucket_owner, live, mine)[None]


def solution(mesh):
    in_specs = (
        P("roll", "tp", None),
        P("roll"),
        P(),
        P("roll", None, "tp"),
        P("roll", None, None, "tp"),
        P("roll", None, "tp"),
        P(None, None, "tp"),
        P(None, "tp"),
        P(None, "tp"),
        P(),
        P(),
    )
    out_specs = P("roll", "tp", None)
    return jax.shard_map(body, mesh=mesh, in_specs=in_specs, out_specs=out_specs, check_vma=False)
```

```python
import jax
import jax.numpy as jnp
from jax import lax
from jax.experimental import pallas as pl
from jax.experimental.pallas import tpu as pltpu
from jax.sharding import PartitionSpec as P

CH = 64
NG = 4
ROWS = CH * NG
F32 = jnp.float32
BF16 = jnp.bfloat16
HIGHEST = lax.Precision.HIGHEST


def mm(a, b):
    return jnp.dot(a, b, preferred_element_type=F32)


def mm_nt(a, b):
    return lax.dot_general(a, b, (((1,), (1,)), ((), ())), preferred_element_type=F32)


def mm_tn(a, b):
    return lax.dot_general(a, b, (((0,), (0,)), ((), ())), preferred_element_type=F32)


def mm_exact(a, b):
    return jnp.dot(a, b, preferred_element_type=F32, precision=HIGHEST)


def silu(v):
    return v / (1.0 + jnp.exp(-v))


def prep_kernel(owner_ref, x_ref, gain_ref, out_ref, scr, inverse):
    x = x_ref[...].astype(F32)
    scale = lax.rsqrt(jnp.mean(x * x, axis=-1, keepdims=True) + 1e-6)
    scr[...] = x * scale * gain_ref[...]
    for b in range(32):
        inverse[owner_ref[b]] = b
    low = lax.broadcasted_iota(jnp.int32, (128, 128), 1) < 64

    def half(block, side):
        tile = scr[:, pl.ds(pl.multiple_of((block // 2) * 128, 128), 128)]
        return jnp.where(block % 2 == side, tile, pltpu.roll(tile, 64, axis=1))

    for j in range(16):
        out_ref[:, j * 128 : (j + 1) * 128] = jnp.where(
            low, half(inverse[2 * j], 0), half(inverse[2 * j + 1], 1)
        ).astype(BF16)


def prep(owner, x, gain):
    return pl.pallas_call(
        prep_kernel,
        out_shape=jax.ShapeDtypeStruct(x.shape, BF16),
        in_specs=[
            pl.BlockSpec(memory_space=pltpu.SMEM),
            pl.BlockSpec(memory_space=pltpu.VMEM),
            pl.BlockSpec(memory_space=pltpu.VMEM),
        ],
        out_specs=pl.BlockSpec(memory_space=pltpu.VMEM),
        scratch_shapes=[pltpu.VMEM(x.shape, F32), pltpu.SMEM((32,), jnp.int32)],
        name="prep",
    )(owner, x, gain)


def finish_kernel(owner_ref, live_ref, x_ref, out_ref, scr):
    scr[...] = x_ref[...].astype(F32)
    live = lax.broadcasted_iota(jnp.int32, (128, 128), 0) < live_ref[0]
    low = lax.broadcasted_iota(jnp.int32, (128, 128), 1) < 64

    def half(block, side):
        tile = scr[:, pl.ds(pl.multiple_of((block // 2) * 128, 128), 128)]
        return jnp.where(block % 2 == side, tile, pltpu.roll(tile, 64, axis=1))

    for j in range(16):
        tile = jnp.where(low, half(owner_ref[2 * j], 0), half(owner_ref[2 * j + 1], 1))
        out_ref[:, j * 128 : (j + 1) * 128] = jnp.where(live, tile, 0.0).astype(BF16)


def finish(owner, live, x):
    return pl.pallas_call(
        finish_kernel,
        out_shape=jax.ShapeDtypeStruct(x.shape, BF16),
        in_specs=[
            pl.BlockSpec(memory_space=pltpu.SMEM),
            pl.BlockSpec(memory_space=pltpu.SMEM),
            pl.BlockSpec(memory_space=pltpu.VMEM),
        ],
        out_specs=pl.BlockSpec(memory_space=pltpu.VMEM),
        scratch_shapes=[pltpu.VMEM(x.shape, F32)],
        name="finish",
    )(owner, live, x)


MESH = pl.DeviceIdType.MESH


class Place:
    def __init__(self):
        roll, tp = lax.axis_index("roll"), lax.axis_index("tp")
        self.zl, self.x, self.core = roll // 8, (roll // 2) % 4, roll % 2
        self.zh, self.y = tp // 4, tp % 4

    def at(self, zl=None, x=None, core=None, zh=None, y=None):
        zl = self.zl if zl is None else zl
        x = self.x if x is None else x
        core = self.core if core is None else core
        zh = self.zh if zh is None else zh
        y = self.y if y is None else y
        return (zl * 8 + x * 2 + core, zh * 4 + y)

    def along_z(self, hops):
        z = (self.zh * 4 + self.zl + hops) % 8
        return self.at(zl=z % 4, zh=z // 4)


def meet(devices):
    barrier = pltpu.get_barrier_semaphore()
    for device in devices:
        pl.semaphore_signal(barrier, inc=1, device_id=device, device_id_type=MESH)
    pl.semaphore_wait(barrier, len(devices))


class Pull:
    def __init__(self, x_ref, w_refs, xo, wos, transit, zs_up, zs_dn, zr, ws, wr, ys, yr, own_sem):
        self.x_ref, self.w_refs, self.xo, self.wos, self.transit = x_ref, w_refs, xo, wos, transit
        self.zs_up, self.zs_dn, self.zr, self.ws, self.wr = zs_up, zs_dn, zr, ws, wr
        self.ys, self.yr, self.own_sem = ys, yr, own_sem
        me = self.me = Place()
        self.xl, self.xr, self.xf = (me.x + 3) % 4, (me.x + 1) % 4, (me.x + 2) % 4
        self.yl, self.yn, self.yf = (me.y + 3) % 4, (me.y + 1) % 4, (me.y + 2) % 4
        self.left_x, self.right_x = me.at(x=self.xl), me.at(x=self.xr)
        self.left_y, self.right_y = me.at(y=self.yl), me.at(y=self.yn)
        self.up, self.down = me.at(zl=(me.zl + 1) % 4), me.at(zl=(me.zl + 3) % 4)
        self.sibling, self.partner = me.at(core=1 - me.core), me.at(zh=1 - me.zh)
        self.behind, self.ahead = me.along_z(6), me.along_z(2)
        self.away_to = me.along_z(jnp.where(me.zh == 0, 6, 2))
        self.outer = (me.zh * 4 + me.zl + 2) % 8 < 4
        self.other = 1 - me.zh
        order = [[0, 1, 2, 3], [1, 2, 0, 3], [2, 1, 3, 0], [3, 2, 1, 0]]
        self.slot = [
            jnp.where(
                me.zl == 0,
                order[0][j],
                jnp.where(me.zl == 1, order[1][j], jnp.where(me.zl == 2, order[2][j], order[3][j])),
            )
            for j in range(4)
        ]

    def meet(self):
        meet(
            [self.left_x, self.right_x, self.left_y, self.right_y, self.up, self.down]
            + [self.sibling, self.partner, self.behind, self.ahead]
        )

    def copy(self, src, dst, send, recv, device):
        return pltpu.make_async_remote_copy(
            src_ref=src, dst_ref=dst, send_sem=send, recv_sem=recv, device_id=device, device_id_type=MESH
        )

    def shard(self, w, z, x, core):
        return self.wos[w].at[pl.ds(pl.multiple_of((z * 8 + x * 2 + core) * 64, 64), 64)]

    def part(self, w, z, x, core, p):
        return self.wos[w].at[pl.ds(pl.multiple_of((z * 8 + x * 2 + core) * 64 + p * 32, 32), 32)]

    def z_copy(self, w, z, src, upward):
        i = w * 4 + z
        dst = self.shard(w, z, self.me.x, self.me.core)
        sems, device = (self.zs_up, self.up) if upward else (self.zs_dn, self.down)
        return self.copy(src, dst, sems.at[i], self.zr.at[i], device)

    def start_z(self, w):
        for upward, has in ((True, self.me.zl < 3), (False, self.me.zl > 0)):

            @pl.when(has)
            def _():
                self.z_copy(w, self.me.zl, self.w_refs[w], upward).start()

    def take_z(self, w, j):
        me, z = self.me, self.slot[j]
        here = self.shard(w, z, me.x, me.core)
        self.z_copy(w, z, here, True).wait_recv()
        for upward, on in ((True, (z < me.zl) & (me.zl < 3)), (False, (z > me.zl) & (me.zl > 0))):

            @pl.when(on)
            def _():
                self.z_copy(w, z, self.shard(w, z, me.x, me.core), upward).start()

    def w_msg(self, w, j, i):
        me, z = self.me, self.slot[j]
        own = self.shard(w, z, me.x, me.core)
        src, dst, device = (
            (self.w_refs[w] if j == 0 else own, own, self.right_x),
            (self.w_refs[w] if j == 0 else own, own, self.left_x),
            (self.part(w, z, self.xl, me.core, 0),) * 2 + (self.right_x,),
            (self.part(w, z, self.xr, me.core, 1),) * 2 + (self.left_x,),
            (self.w_refs[w] if j == 0 else own, own, self.sibling),
            (self.shard(w, z, self.xl, me.core),) * 2 + (self.sibling,),
            (self.shard(w, z, self.xr, me.core),) * 2 + (self.sibling,),
            (self.shard(w, z, self.xf, me.core),) * 2 + (self.sibling,),
        )[i]
        n = w * 32 + j * 8 + i
        return self.copy(src, dst, self.ws.at[n], self.wr.at[n], device)

    def w_wait(self, w, j, i):
        me, z = self.me, self.slot[j]
        dst = (
            lambda: self.shard(w, z, self.xl, me.core),
            lambda: self.shard(w, z, self.xr, me.core),
            lambda: self.part(w, z, self.xf, me.core, 0),
            lambda: self.part(w, z, self.xf, me.core, 1),
            lambda: self.shard(w, z, me.x, 1 - me.core),
            lambda: self.shard(w, z, self.xl, 1 - me.core),
            lambda: self.shard(w, z, self.xr, 1 - me.core),
            lambda: self.shard(w, z, self.xf, 1 - me.core),
        )[i]()
        n = w * 32 + j * 8 + i
        self.copy(dst, dst, self.ws.at[n], self.wr.at[n], self.sibling).wait_recv()

    def spread_x(self, w, j):
        for i in (0, 1, 4):
            self.w_msg(w, j, i).start()

    def relay_x(self, w, j):
        self.w_wait(w, j, 0)
        self.w_msg(w, j, 2).start()
        self.w_wait(w, j, 1)
        self.w_msg(w, j, 3).start()
        self.w_msg(w, j, 5).start()
        self.w_msg(w, j, 6).start()

    def far_x(self, w, j):
        self.w_wait(w, j, 2)
        self.w_wait(w, j, 3)
        self.w_msg(w, j, 7).start()

    def siblings(self, w):
        for j in range(4):
            for i in range(4, 8):
                self.w_wait(w, j, i)

    def block(self, zh, y, p):
        return self.xo.at[pl.ds(pl.multiple_of((zh * 4 + y) * 128 + p * 64, 64), 64)]

    def y_msg(self, b, k):
        me = self.me
        zh = self.other if b else me.zh
        if k < 4:
            dst = self.block(zh, me.y, k % 2)
            src = dst if b else self.x_ref.at[pl.ds(k % 2 * 64, 64)]
            device = self.right_y if k < 2 else self.left_y
        else:
            dst = src = self.block(zh, self.yl if k == 4 else self.yn, k - 4)
            device = self.right_y if k == 4 else self.left_y
        return self.copy(src, dst, self.ys.at[b * 6 + k], self.yr.at[b * 6 + k], device)

    def y_wait(self, b, k):
        zh = self.other if b else self.me.zh
        y, p = ((self.yl, 0), (self.yl, 1), (self.yn, 0), (self.yn, 1), (self.yf, 0), (self.yf, 1))[k]
        dst = self.block(zh, y, p)
        self.copy(dst, dst, self.ys.at[b * 6 + k], self.yr.at[b * 6 + k], self.partner).wait_recv()

    def relay_y(self, b):
        self.y_wait(b, 0)
        self.y_msg(b, 4).start()
        self.y_wait(b, 3)
        self.y_msg(b, 5).start()

    def rest_y(self, b):
        for k in (1, 2, 4, 5):
            self.y_wait(b, k)

    def direct(self):
        return self.copy(
            self.x_ref.at[pl.ds(0, 64)], self.block(self.me.zh, self.me.y, 0), self.ys.at[12], self.yr.at[12], self.partner
        )

    def away(self):
        i = 13 + 2 * self.me.zh
        return self.copy(
            self.x_ref.at[pl.ds(64, 64)], self.transit.at[self.me.zh], self.ys.at[i], self.yr.at[i], self.away_to
        )

    def onward(self, s):
        i = 14 + 2 * s
        return self.copy(
            self.transit.at[s], self.block(s, self.me.y, 1), self.ys.at[i], self.yr.at[i], self.ahead if s else self.behind
        )

    def pass_on(self):
        @pl.when(self.outer)
        def _():
            for s in range(2):
                i = 13 + 2 * s
                dst = self.transit.at[s]
                self.copy(dst, dst, self.ys.at[i], self.yr.at[i], self.partner).wait_recv()
                self.onward(s).start()

    def take_other(self, p):
        i = 14 + 2 * self.other if p else 12
        dst = self.block(self.other, self.me.y, p)
        self.copy(dst, dst, self.ys.at[i], self.yr.at[i], self.partner).wait_recv()
        self.y_msg(1, p).start()
        self.y_msg(1, 2 + p).start()

    def open(self):
        me = self.me
        self.meet()
        self.start_z(0)
        self.spread_x(0, 0)
        self.away().start()
        self.direct().start()
        for k in (0, 2, 1, 3):
            self.y_msg(0, k).start()
        keep = [
            pltpu.make_async_copy(self.w_refs[w], self.shard(w, me.zl, me.x, me.core), self.own_sem.at[w])
            for w in range(2)
        ]
        rows = pl.ds(pl.multiple_of((me.zh * 4 + me.y) * 128, 128), 128)
        keep.append(pltpu.make_async_copy(self.x_ref, self.xo.at[rows], self.own_sem.at[2]))
        for c in keep:
            c.start()
        for j in (1, 2, 3):
            self.take_z(0, j)
            self.spread_x(0, j)
            self.relay_x(0, j - 1)
            if j == 2:
                self.relay_y(0)
                self.pass_on()
        self.start_z(1)
        self.far_x(0, 0)
        self.take_other(0)
        self.far_x(0, 1)
        self.take_other(1)
        self.relay_x(0, 3)
        self.take_z(1, 1)
        self.far_x(0, 2)
        self.take_z(1, 2)

        @pl.when(me.zh == 1)
        def _():
            self.relay_y(1)

        self.far_x(0, 3)
        self.take_z(1, 3)
        for j in range(4):
            self.spread_x(1, j)

        @pl.when(me.zh == 0)
        def _():
            self.rest_y(0)

        @pl.when(me.zh == 1)
        def _():
            self.rest_y(1)

        self.siblings(0)
        for c in keep:
            c.wait()

    def second(self):
        @pl.when(self.me.zh == 0)
        def _():
            self.relay_y(1)

        for j in range(4):
            self.relay_x(1, j)

    def third(self):
        for j in range(4):
            self.far_x(1, j)

    def later_half(self):
        @pl.when(self.me.zh == 0)
        def _():
            self.rest_y(1)

        @pl.when(self.me.zh == 1)
        def _():
            self.rest_y(0)

    def close(self):
        me = self.me
        for w in range(2):
            for j in range(4):
                z = self.slot[j]
                for i in range(8):
                    self.w_msg(w, j, i).wait_send()
                for upward, on in ((True, (z <= me.zl) & (me.zl < 3)), (False, (z >= me.zl) & (me.zl > 0))):

                    @pl.when(on)
                    def _():
                        self.z_copy(w, z, self.shard(w, z, me.x, me.core), upward).wait_send()

        for b in range(2):
            for k in range(6):
                self.y_msg(b, k).wait_send()
        self.direct().wait_send()
        self.away().wait_send()

        @pl.when(self.outer)
        def _():
            for s in range(2):
                self.onward(s).wait_send()


DMA = pltpu.SemaphoreType.DMA


class Sums:
    def __init__(self, p_ref, first, full, mixed, kept, summed, landed, transit, ss, rs):
        self.p, self.first, self.full, self.mixed = p_ref, first, full, mixed
        self.kept, self.summed, self.landed, self.transit = kept, summed, landed, transit
        self.ss, self.rs = ss, rs
        me = self.me = Place()
        self.left, self.right = me.at(y=(me.y + 3) % 4), me.at(y=(me.y + 1) % 4)
        self.partner, self.behind, self.ahead = me.at(zh=1 - me.zh), me.along_z(6), me.along_z(2)
        self.outer = (me.zh * 4 + me.zl + 2) % 8 < 4

    def copy(self, i, src, dst, device):
        return pltpu.make_async_remote_copy(
            src_ref=src, dst_ref=dst, send_sem=self.ss.at[i], recv_sem=self.rs.at[i], device_id=device, device_id_type=MESH
        )

    def half(self, b, y, p):
        return self.p.at[pl.ds(pl.multiple_of((b * 4 + y) * 128 + p * 64, 64), 64)]

    def message(self, b, k):
        y, first, full = self.me.y, self.first, self.full
        far, right, left = (y + 2) % 4, (y + 1) % 4, (y + 3) % 4
        src, dst = (
            (self.half(b, far, 0), first.at[b, 0]),
            (self.half(b, far, 1), first.at[b, 1]),
            (self.half(b, right, 1), full.at[b, 0, 1]),
            (self.half(b, left, 0), full.at[b, 1, 0]),
            (self.mixed.at[b, 0], full.at[b, 0, 0]),
            (self.mixed.at[b, 1], full.at[b, 1, 1]),
        )[k]
        return self.copy(b * 6 + k, src, dst, self.left if k % 2 else self.right)

    def begin(self, b):
        for k in range(4):
            self.message(b, k).start()

    def begin_blocks(self, b, upper):
        y = self.me.y
        for k, block in enumerate(((y + 2) % 4, (y + 2) % 4, (y + 1) % 4, (y + 3) % 4)):

            @pl.when((block >= 2) if upper else (block < 2))
            def _():
                self.message(b, k).start()

    def relay_part(self, b, p, near):
        self.message(b, p).wait_recv()
        self.mixed[b, p] = (self.half(b, near, p)[...].astype(F32) + self.first[b, p].astype(F32)).astype(BF16)
        self.message(b, 4 + p).start()

    def relay(self, b):
        y = self.me.y
        for p, near in ((0, (y + 1) % 4), (1, (y + 3) % 4)):
            self.relay_part(b, p, near)

    def relay_blocks(self, b, upper):
        y = self.me.y
        for p, near in ((0, (y + 1) % 4), (1, (y + 3) % 4)):

            @pl.when((near >= 2) if upper else (near < 2))
            def _():
                self.relay_part(b, p, near)

    def across(self, b, p):
        if p == 0:
            return self.copy(12, self.summed.at[0], self.landed.at[0], self.partner)
        return self.copy(13 + 2 * b, self.summed.at[1], self.transit.at[b], self.behind if b else self.ahead)

    def passing(self, b):
        return self.copy(14 + 2 * b, self.transit.at[b], self.landed.at[1], self.behind if b else self.ahead)

    def total(self, b):
        for p in (1, 0):
            for k in ((3, 4), (2, 5))[p]:
                self.message(b, k).wait_recv()
            value = (
                self.half(b, self.me.y, p)[...].astype(F32)
                + self.full[b, 0, p].astype(F32)
                + self.full[b, 1, p].astype(F32)
            )

            @pl.when(self.me.zh == b)
            def _():
                self.kept[p] = value

            @pl.when(self.me.zh != b)
            def _():
                self.summed[p] = value.astype(BF16)
                self.across(b, p).start()

    def pass_on(self, b):
        @pl.when(self.outer)
        def _():
            self.across(b, 1).wait_recv()
            self.passing(b).start()

    def finish(self, out_ref):
        self.across(0, 0).wait_recv()
        for b in range(2):

            @pl.when(self.me.zh == b)
            def _():
                self.passing(b).wait_recv()

        for p in range(2):
            out_ref[p * 64 : (p + 1) * 64, :] = (self.kept[p] + self.landed[p].astype(F32)).astype(BF16)
        for b in range(2):
            for k in range(6):
                self.message(b, k).wait_send()
        self.across(0, 0).wait_send()
        for b in range(2):

            @pl.when(self.me.zh != b)
            def _():
                self.across(b, 1).wait_send()

            @pl.when(self.outer)
            def _():
                self.passing(b).wait_send()


def mixer_kernel(
    own_ref, w1_ref, w2_ref, taps_ref, rate_ref, bias_ref, gain_ref, out_ref,
    x_ref, w_ref, wout_ref, hid, passing, zs_up, zs_dn, zr, ws, wr, ys, yr, own_sem,
    pscr, oscr, state, p_ref, first, full, mixed, kept, summed, landed, transit, ss, rs,
):
    step = pl.program_id(0)
    across = Sums(p_ref, first, full, mixed, kept, summed, landed, transit, ss, rs)

    pull = Pull(
        own_ref, (w1_ref, w2_ref), x_ref, (w_ref, wout_ref), passing, zs_up, zs_dn, zr, ws, wr, ys, yr, own_sem
    )

    @pl.when(step == 0)
    def _():
        pull.open()

    @pl.when(step == 1)
    def _():
        pull.second()

    @pl.when(step == 2)
    def _():
        across.begin(0)
        pull.later_half()


    @pl.when(step == 0)
    def _():
        pscr[0:8, :] = jnp.zeros((8, 1024), F32)
        state[...] = jnp.zeros_like(state)

    @pl.when(step > 0)
    def _():
        pscr[0:8, :] = pscr[ROWS : ROWS + 8, :]

    here = pl.ds(pl.multiple_of(step * ROWS, ROWS), ROWS)
    x = x_ref[here, :]
    gates = mm(x, w_ref[:, 1536:1664])
    pscr[8 : 8 + ROWS, :] = mm(x, w_ref[:, 0:1024])

    @pl.when(step == 1)
    def _():
        pull.third()


    lane = lax.broadcasted_iota(jnp.int32, (1, 128), 1)
    rate, bias = jnp.zeros((1, 128), F32), jnp.zeros((1, 128), F32)
    for n in range(4):
        rate = jnp.where(lane == n, rate_ref[n // 2, n % 2], rate)
        bias = jnp.where(lane == n, bias_ref[n // 2, n % 2], bias)
    biased = gates + bias
    soft = jnp.maximum(biased, 0.0) + jnp.log(1.0 + jnp.exp(-jnp.abs(biased)))
    beta = 1.0 / (1.0 + jnp.exp(-gates))
    is_decay, is_beta = lane < 4, (lane >= 4) & (lane < 8)
    ri = lax.broadcasted_iota(jnp.int32, (ROWS, ROWS), 0)
    ci = lax.broadcasted_iota(jnp.int32, (ROWS, ROWS), 1)
    same = (ri // CH) == (ci // CH)
    tri = jnp.where(same & (ri >= ci), 1.0, 0.0).astype(BF16)

    def thirds(v):
        hi = v.astype(BF16).astype(F32)
        rest = v - hi
        mid = rest.astype(BF16).astype(F32)
        return (hi + pltpu.roll(mid, 8, axis=1) + pltpu.roll(rest - mid, 16, axis=1)).astype(BF16)

    sums = mm(tri, thirds(jnp.where(is_decay, -rate * soft, 0.0)))
    sums = sums + pltpu.roll(sums, 120, axis=1) + pltpu.roll(sums, 112, axis=1)
    both = thirds(jnp.where(is_decay, sums, jnp.where(is_beta, beta, 0.0)))

    def spread(first, width):
        r = lax.broadcasted_iota(jnp.int32, (128, 4 * width), 0)
        c = lax.broadcasted_iota(jnp.int32, (128, 4 * width), 1)
        return jnp.where((r < 24) & (r % 8 == c // width + first), 1.0, 0.0).astype(BF16)

    tot_w = mm(both, spread(0, CH))
    beta_w = mm(both, spread(4, CH))
    tot_v = mm(both, spread(0, 128))
    beta_v = mm(both, spread(4, 128))
    grow_v = jnp.exp(tot_v)

    mixed = []
    taps = [taps_ref[i].astype(F32) for i in range(4)]
    for c in range(4):
        acc = None
        for i in range(4):
            term = taps[i][c : c + 1] * pscr[8 - i : 8 - i + ROWS, c * 256 : (c + 1) * 256]
            acc = term if acc is None else acc + term
        mixed.append(silu(acc))

    def unit(v):
        parts = []
        for h in range(2):
            p = v[:, h * 128 : (h + 1) * 128]
            parts.append(p * lax.rsqrt(jnp.sum(p * p, axis=-1, keepdims=True) + 1e-6))
        return jnp.concatenate(parts, axis=1)

    query = (unit(mixed[0]) * (128.0 ** -0.5)).astype(BF16)
    keys_f = unit(mixed[1])
    keys = keys_f.astype(BF16)

    wi = lax.broadcasted_iota(jnp.int32, (CH, 256), 0)
    wj = lax.broadcasted_iota(jnp.int32, (CH, 256), 1) % CH
    eye = wi == wj
    lower = wi >= wj
    strict = wi > wj
    bd_mask = same
    kmask = (lax.broadcasted_iota(jnp.int32, (128, 256), 0) // CH) == (
        lax.broadcasted_iota(jnp.int32, (128, 256), 1) // 128
    )

    def bd(v):
        vb = v.astype(BF16)
        return jnp.where(bd_mask, jnp.concatenate([vb] * 4, axis=0), jnp.zeros((), BF16))

    chunks = range(NG)
    rows = [slice(c * CH, (c + 1) * CH) for c in chunks]
    sys_w, score_w = [], []
    for c in chunks:
        k_c, q_c = keys[rows[c]], query[rows[c]]
        k_bd = jnp.where(kmask, jnp.concatenate([k_c, k_c], axis=0), jnp.zeros((), BF16))
        both = mm_nt(jnp.concatenate([k_c, q_c], axis=0), k_bd)
        kk = jnp.concatenate([both[:CH], both[:CH]], axis=1)
        qk = jnp.concatenate([both[CH:], both[CH:]], axis=1)
        t_c = tot_w[rows[c]]
        t_row = jnp.sum(jnp.where(eye, t_c, 0.0), axis=0, keepdims=True)
        inside = jnp.where(lower, jnp.exp(jnp.where(lower, t_c - t_row, 0.0)), 0.0)
        sys_w.append(jnp.where(strict, beta_w[rows[c]] * kk * inside, 0.0))
        score_w.append(qk * inside)

    eye_f = jnp.where(eye, 1.0, 0.0)

    def block(n):
        return (wi // n) == (wj // n)

    base = [jnp.where(block(8), a, 0.0) for a in sys_w]
    base2 = [mm(d.astype(BF16), bd(d)) for d in base]
    base4 = [mm(d.astype(BF16), bd(d)) for d in base2]
    inv = [eye_f - d for d in base]
    inv = [t + mm(t.astype(BF16), bd(d)) for t, d in zip(inv, base2)]
    inv = [t + mm(t.astype(BF16), bd(d)) for t, d in zip(inv, base4)]
    for n in (16, 32, 64):
        pick = block(n) & jnp.logical_not(block(n // 2))
        low = [jnp.where(pick, a, 0.0).astype(BF16) for a in sys_w]
        mid = [mm(l, bd(t)) for l, t in zip(low, inv)]
        inv = [t - mm(t.astype(BF16), bd(m)) for t, m in zip(inv, mid)]
    fixed = []
    for c in chunks:
        a_hi = sys_w[c].astype(BF16)
        a_lo = (sys_w[c] - a_hi.astype(F32)).astype(BF16)
        t_hi = inv[c].astype(BF16)
        t_lo = (inv[c] - t_hi.astype(F32)).astype(BF16)
        both = mm(jnp.concatenate([a_hi, a_lo], axis=0), bd(t_hi))
        prod = both[:CH] + both[CH:] + mm(a_hi, bd(t_lo))
        resid = eye_f - inv[c] - prod
        fixed.append(inv[c] + mm(t_hi, bd(resid)))
    inv = fixed

    solved = []
    for c in chunks:
        parts = []
        for s in range(2):
            for h in range(2):
                n = s * 2 + h
                b = beta_v[rows[c], n * 128 : (n + 1) * 128]
                g = grow_v[rows[c], n * 128 : (n + 1) * 128]
                v = mixed[2 + s][rows[c], h * 128 : (h + 1) * 128]
                k = keys_f[rows[c], h * 128 : (h + 1) * 128]
                parts.append(jnp.concatenate([(b * v).astype(BF16), (b * g * k).astype(BF16)], axis=1))
        rhs = jnp.concatenate(parts, axis=0)
        solved.append(mm(bd(inv[c]), rhs))
    score_bd = [bd(s) for s in score_w]

    for c in chunks:
        reads = []
        for h in range(2):
            lhs = jnp.concatenate(
                [
                    solved[c][h * CH : (h + 1) * CH, 128:256].astype(BF16),
                    solved[c][(2 + h) * CH : (3 + h) * CH, 128:256].astype(BF16),
                    query[rows[c], h * 128 : (h + 1) * 128],
                ],
                axis=0,
            )
            reads.append(mm(lhs, state[h].astype(BF16)))
        updates, writes = [None] * 4, [None] * 4
        last = tot_v[(c + 1) * CH - 1 : (c + 1) * CH, :]
        for s in range(2):
            for h in range(2):
                n = s * 2 + h
                u = solved[c][n * CH : (n + 1) * CH, 0:128] - reads[h][s * CH : (s + 1) * CH, s * 128 : (s + 1) * 128]
                carry = jnp.exp(last[:, n * 128 : (n + 1) * 128] - tot_v[rows[c], n * 128 : (n + 1) * 128])
                updates[n] = u.astype(BF16)
                writes[n] = (carry * u).astype(BF16)
        for h in range(2):
            decay_all = jnp.concatenate(
                [jnp.exp(last[:, h * 128 : (h + 1) * 128]), jnp.exp(last[:, (2 + h) * 128 : (3 + h) * 128])], axis=1
            )
            write = jnp.concatenate([writes[h], writes[2 + h]], axis=1)
            state[h] = decay_all * state[h] + mm_tn(keys[rows[c], h * 128 : (h + 1) * 128], write)
        inner = mm(score_bd[c], jnp.concatenate(updates, axis=0))
        for s in range(2):
            for h in range(2):
                n = s * 2 + h
                oscr[rows[c], n * 128 : (n + 1) * 128] = (
                    grow_v[rows[c], n * 128 : (n + 1) * 128] * reads[h][2 * CH :, s * 128 : (s + 1) * 128]
                    + inner[n * CH : (n + 1) * CH]
                )

    og = mm(x, w_ref[:, 1024:1536])
    hidden = []
    for n in range(4):
        r = oscr[:, n * 128 : (n + 1) * 128]
        r = r * lax.rsqrt(jnp.mean(r * r, axis=-1, keepdims=True) + 1e-6) * gain_ref[...]
        hidden.append((r * silu(og[:, n * 128 : (n + 1) * 128])).astype(BF16))
    hidden = jnp.concatenate(hidden, axis=1)
    hid[here, :] = hidden


    @pl.when(step == 1)
    def _():
        pull.siblings(1)
        p_ref[0:ROWS, :] = mm_nt(hid[0:ROWS, :], wout_ref[...]).astype(BF16)

    @pl.when(step > 0)
    def _():
        p_ref[here, :] = mm_nt(hid[here, :], wout_ref[...]).astype(BF16)

    @pl.when(step == 2)
    def _():
        across.relay(0)
        across.begin_blocks(1, False)

    @pl.when(step == 3)
    def _():
        across.begin_blocks(1, True)
        across.relay_blocks(1, False)
        across.total(0)
        across.relay_blocks(1, True)
        across.pass_on(0)
        across.total(1)
        across.pass_on(1)
        across.finish(out_ref)
        pull.close()


def mixer(rows, w1, w2, taps, rate, bias, gain):
    own, width = rows.shape
    seq, depth = own * 8, w1.shape[0] * 32
    whole = lambda i: (0, 0)
    return pl.pallas_call(
        mixer_kernel,
        grid=(seq // ROWS,),
        out_shape=jax.ShapeDtypeStruct(rows.shape, BF16),
        in_specs=[
            pl.BlockSpec(memory_space=pl.ANY),
            pl.BlockSpec(memory_space=pl.ANY),
            pl.BlockSpec(memory_space=pl.ANY),
            pl.BlockSpec((4, 4, 256), lambda i: (0, 0, 0)),
            pl.BlockSpec(memory_space=pltpu.SMEM),
            pl.BlockSpec(memory_space=pltpu.SMEM),
            pl.BlockSpec((1, 128), whole),
        ],
        out_specs=pl.BlockSpec(rows.shape, whole),
        scratch_shapes=[
            pltpu.VMEM((seq, width), BF16),
            pltpu.VMEM((depth, w1.shape[1]), BF16),
            pltpu.VMEM((depth, w2.shape[1]), BF16),
            pltpu.VMEM((seq, 512), BF16),
            pltpu.VMEM((2, 64, width), BF16),
            DMA((8,)), DMA((8,)), DMA((8,)),
            DMA((64,)), DMA((64,)),
            DMA((17,)), DMA((17,)),
            DMA((3,)),
            pltpu.VMEM((ROWS + 8, 1024), F32),
            pltpu.VMEM((ROWS, 512), F32),
            pltpu.VMEM((2, 128, 256), F32),
            pltpu.VMEM((seq, width), BF16),
            pltpu.VMEM((2, 2, 64, width), BF16),
            pltpu.VMEM((2, 2, 2, 64, width), BF16),
            pltpu.VMEM((2, 2, 64, width), BF16),
            pltpu.VMEM((2, 64, width), F32),
            pltpu.VMEM((2, 64, width), BF16),
            pltpu.VMEM((2, 64, width), BF16),
            pltpu.VMEM((2, 64, width), BF16),
            DMA((17,)), DMA((17,)),
        ],
        compiler_params=pltpu.CompilerParams(collective_id=0, has_side_effects=True, vmem_limit_bytes=58 << 20),
        name="mixer",
    )(rows, w1, w2, taps, rate, bias, gain)


def body(
    prompt_states,
    lengths,
    bucket_owner,
    w_in,
    w_gates,
    out_weight,
    conv_weight,
    decay_rate,
    dt_bias,
    in_gain,
    head_gain,
):
    tok_rows = prompt_states.shape[1]
    rows = w_in.shape[0]
    normed = prep(bucket_owner, prompt_states[0], in_gain[None, :])
    packed = jnp.concatenate(
        [w_in.reshape(rows, -1), jnp.pad(w_gates.reshape(rows, -1), ((0, 0), (0, 120)))], axis=1
    )
    mine = mixer(
        normed, packed, out_weight.reshape(rows, -1), conv_weight, decay_rate, dt_bias, head_gain[None, :]
    )
    live = lengths - lax.axis_index("tp") * tok_rows
    return finish(bucket_owner, live, mine)[None]


def solution(mesh):
    in_specs = (
        P("roll", "tp", None),
        P("roll"),
        P(),
        P("roll", None, "tp"),
        P("roll", None, None, "tp"),
        P("roll", None, "tp"),
        P(None, None, "tp"),
        P(None, "tp"),
        P(None, "tp"),
        P(),
        P(),
    )
    out_specs = P("roll", "tp", None)
    return jax.shard_map(body, mesh=mesh, in_specs=in_specs, out_specs=out_specs, check_vma=False)
```
